32 devices in a mesh: row: 4 (over y, core), col: 8 (over z, x).
Axes of the slice: x: 2, y: 2, z: 4, core: 2. Of those that a mesh axis runs over, the one named last changes fastest.
Arguments:
- positions: float32 [3, 512], P(None, ('row', 'col')), as said below
- thermal_noise: float32 [32, 3, 512], P(None, None, ('row', 'col')), as said below
Outputs:
- displacement: float32 [32, 3, 512], P(None, None, ('row', 'col'))
Inputs may be any that keep to these rules, and one draw needn't show every extreme that they name: `positions`: any two particles are at least 1.0 apart. `thermal_noise`: finite real entries.
All inputs are finite; a program needn't handle non-finite values.
Results may differ from the reference program's by a relative error of at most 0.0013.
Values may be sent and summed in bfloat16 or wider, within the bound.
A program may use at most 64 MiB of HBM per device.

```python
import math
import jax
import jax.numpy as jnp
from jax import lax

SAMPLES = 32
PARTICLES = 512


def draw_positions(key, part):
    lattice_side = 1
    while lattice_side ** 3 < PARTICLES:
        lattice_side = lattice_side + 1
    cells = jax.random.permutation(jax.random.fold_in(key, 11), lattice_side ** 3)[:PARTICLES]
    lattice = jnp.stack([cells // (lattice_side * lattice_side), cells // lattice_side % lattice_side, cells % lattice_side]).astype(jnp.float32)
    jitter = jax.random.uniform(jax.random.fold_in(key, 14), (3, PARTICLES), jnp.float32, -0.3, 0.3)
    return (2.5 * (lattice + jitter)).astype(jnp.float32)


def draw_thermal_noise(key, part):
    ramp = jnp.arange(PARTICLES, dtype=jnp.float32) / PARTICLES
    gaussian = jax.random.normal(jax.random.fold_in(key, 21), (SAMPLES, 3, PARTICLES), jnp.float32)
    return (gaussian * jnp.exp(0.5 * ramp * math.log(3.0))).astype(jnp.float32)


def setup_inputs(seed: int = 0) -> dict:
    key_list = jax.random.split(jax.random.key(seed), 3)
    return {
        "positions": draw_positions(jax.random.fold_in(key_list[2], 71), 0),
        "thermal_noise": draw_thermal_noise(jax.random.fold_in(key_list[2], 71), 0),
    }


def pair_tensor(rows_pos, cols_pos, retain):
    offsets = [rows_pos[a][None, :] - cols_pos[a][:, None] for a in range(3)]
    squared = offsets[0] * offsets[0] + offsets[1] * offsets[1] + offsets[2] * offsets[2]
    guarded = jnp.where(retain, squared, 4.0)
    inverse = lax.rsqrt(guarded)
    distance = guarded * inverse
    correlation = distance < 2.0
    inverse_cube = inverse * inverse * inverse
    inverse_fifth = inverse_cube * inverse * inverse
    isotropic = jnp.where(correlation, 1.0 - 0.28125 * distance, 0.75 * inverse + 0.5 * inverse_cube)
    dyadic = jnp.where(correlation, 0.09375 * inverse, 0.75 * inverse_cube - 1.5 * inverse_fifth)
    isotropic = jnp.where(retain, isotropic, 0.0)
    dyadic = jnp.where(retain, dyadic, 0.0)
    columns = []
    for b in range(3):
        elements = []
        for a in range(3):
            element = dyadic * offsets[a] * offsets[b]
            if a == b:
                element = element + isotropic
            elements.append(element)
        columns.append(jnp.stack(elements, axis=1))
    return jnp.stack(columns, axis=0)

def apply_mobility(positions, vector):
    particles = positions.shape[1]
    block_rows = 128
    rounded = vector.astype(jnp.bfloat16)
    rounded = lax.optimization_barrier(rounded).astype(jnp.float32)

    def one_block(row_start):
        rows_pos = lax.dynamic_slice_in_dim(positions, row_start, block_rows, 1)
        row_label = row_start + jnp.arange(block_rows, dtype=jnp.int32)
        col_label = jnp.arange(particles, dtype=jnp.int32)
        retain = row_label[None, :] != col_label[:, None]
        tensor = pair_tensor(rows_pos, positions, retain).astype(jnp.bfloat16)
        tensor = lax.optimization_barrier(tensor).astype(jnp.float32)
        return jnp.einsum('kbj,bjai->kai', rounded, tensor, precision=lax.Precision.HIGHEST)
    block_starts = jnp.arange(particles // block_rows, dtype=jnp.int32) * block_rows
    block_terms = lax.map(one_block, block_starts)
    coupled = jnp.transpose(block_terms, (1, 2, 0, 3)).reshape(vector.shape)
    return vector + coupled

def reference(positions, thermal_noise):
    squares = lax.optimization_barrier(jnp.sum(thermal_noise * thermal_noise, axis=(1, 2)))
    noise_length = jnp.sqrt(squares + 1e-06)
    basis_one = thermal_noise / noise_length[:, None, None]
    image_one = apply_mobility(positions, basis_one)
    alpha_one = lax.optimization_barrier(jnp.sum(basis_one * image_one, axis=(1, 2)))
    remainder = image_one - alpha_one[:, None, None] * basis_one
    beta_one = jnp.sqrt(lax.optimization_barrier(jnp.sum(remainder * remainder, axis=(1, 2))) + 1e-06)
    basis_two = remainder / beta_one[:, None, None]
    image_two = apply_mobility(positions, basis_two)
    alpha_two = lax.optimization_barrier(jnp.sum(basis_two * image_two, axis=(1, 2)))
    det_root = jnp.sqrt(alpha_one * alpha_two - beta_one * beta_one)
    trace_root = jnp.sqrt(alpha_one + alpha_two + 2.0 * det_root)
    weight_one = (alpha_one + det_root) / trace_root
    weight_two = beta_one / trace_root
    return 0.5 * noise_length[:, None, None] * (weight_one[:, None, None] * basis_one + weight_two[:, None, None] * basis_two)
```

```python
import functools

import jax
import jax.numpy as jnp
from jax import lax
from jax.experimental import pallas as pl
from jax.experimental.pallas import tpu as pltpu
from jax.sharding import PartitionSpec as P

LANES = 128
LOGICAL = pl.DeviceIdType.LOGICAL
MUTUAL = 0
BLOCKS = ((0, 0), (1, 1), (2, 2), (0, 1), (0, 2), (1, 2))


def chip_bits(rows, cols):
    bits = [(1, 1)]
    weight = 2
    while weight < rows:
        bits.append((weight * cols, weight // 2))
        weight = 2 * weight
    weight = 2
    while weight < cols:
        bits.append((weight, weight // 2))
        weight = 2 * weight
    return bits


def replicated_kernel(
    rows,
    cols,
    noise_hbm,
    pos_hbm,
    out_ref,
    noise_ref,
    pos_ref,
    gathered,
    stage,
    own_ref,
    noise_full,
    pos_cols,
    pos_rows,
    mobility,
    narrow,
    image,
    load_sem,
    send_sem,
    recv_sem,
    grant,
):
    _, per_device, samples = noise_ref.shape
    particles = rows * cols * per_device
    f32, bf16 = jnp.float32, jnp.bfloat16
    my_row, my_col = lax.axis_index("row"), lax.axis_index("col")

    load_pos = pltpu.make_async_copy(pos_hbm, pos_ref, load_sem.at[0])
    load_noise = pltpu.make_async_copy(noise_hbm, noise_ref, load_sem.at[1])
    load_pos.start()
    load_noise.start()

    bits = chip_bits(rows, cols)
    chips = rows * cols // 2
    me = my_row * cols + my_col
    core = lax.rem(my_row, 2)
    mate = cols * (1 - 2 * core)
    my_code = 0
    device, ahead, level = {0: me}, {0: 0}, {0: 0}
    for index, (weight, height) in enumerate(bits):
        digit = lax.rem(me // weight, 2)
        my_code = my_code + (digit << index)
        sign = 1 - 2 * digit
        for code in range(1 << index):
            device[code + (1 << index)] = device[code] + weight * sign
            ahead[code + (1 << index)] = ahead[code] + height * sign
            level[code + (1 << index)] = level[code] + height
    order = sorted(range(chips), key=lambda code: (level[code], code))

    def both(code):
        return device[code], device[code] + mate

    barrier = pltpu.get_barrier_semaphore()
    pl.semaphore_signal(barrier, inc=1, device_id=me + mate, device_id_type=LOGICAL)
    greetings = 1
    for code in order[1:]:
        greetings = greetings + jnp.where(ahead[code] <= MUTUAL, 2, 0)

        @pl.when(ahead[code] >= -MUTUAL)
        def _(code=code):
            for target in both(code):
                pl.semaphore_signal(barrier, inc=1, device_id=target, device_id_type=LOGICAL)

    stage[...] = jnp.zeros_like(stage)
    own_ref[...] = jnp.zeros_like(own_ref)
    load_pos.wait()
    position = pos_ref[...]
    for term in range(3):
        piece = position.astype(bf16).astype(f32)
        stage[pl.ds(3 * term, 3), pl.ds(0, per_device)] = piece
        position = position - piece
    turned = jnp.transpose(stage[...])
    own_ref[:, pl.ds(3 * samples, 16)] = turned[0:per_device, :]

    pl.semaphore_wait(barrier, greetings)
    for code in order[:0:-1]:

        @pl.when(ahead[code] < -MUTUAL)
        def _(code=code):
            for target in both(code):
                pl.semaphore_signal(
                    grant.at[code], inc=1, device_id=target, device_id_type=LOGICAL
                )

    load_noise.wait()
    for b in range(3):
        own_ref[:, pl.ds(b * samples, samples)] = noise_ref[b]
    gathered[0, 0] = own_ref[...].astype(bf16)

    def send(code, side, target):
        pltpu.make_async_remote_copy(
            src_ref=gathered.at[0, 0],
            dst_ref=gathered.at[code, side],
            send_sem=send_sem.at[code],
            recv_sem=recv_sem.at[code],
            device_id=target,
            device_id_type=LOGICAL,
        ).start()

    def finished(ref, semaphore):
        pltpu.make_async_copy(ref, ref, semaphore).wait()

    @pl.when(my_code > 0)
    def _():
        for side in range(2):
            send(my_code, side, core * cols + side * mate)

    for code in order[:0:-1]:

        @pl.when((ahead[code] <= MUTUAL) & (my_code != code))
        def _(code=code):
            for side, target in enumerate(both(code)):
                send(code, side, target)

    send(0, 1, me + mate)

    def send_later(code):
        @pl.when(ahead[code] > MUTUAL)
        def _():
            pl.semaphore_wait(grant.at[code], 2)
            for side, target in enumerate(both(code)):
                send(code, side, target)

    lane = lax.broadcasted_iota(jnp.int32, (1, LANES), 1)
    field = lax.broadcasted_iota(jnp.int32, (LANES, 3 * LANES), 0) - 3 * samples
    target = lax.broadcasted_iota(jnp.int32, (LANES, 3 * LANES), 1) // LANES
    select = (field == target) | (field == target + 3) | (field == target + 6)
    over_lanes = select.astype(f32).astype(bf16)
    fields = 3 * samples
    field = lax.broadcasted_iota(jnp.int32, (fields + 3 * 16, LANES), 1)
    target = lax.broadcasted_iota(jnp.int32, (fields + 3 * 16, LANES), 0)
    coordinate = (target - fields) // 16
    moved = (field - fields == coordinate) | (field - fields == coordinate + 3)
    moved = moved | (field - fields == coordinate + 6)
    select = ((target < fields) & (field == target)) | ((target >= fields) & moved)
    turning = select.astype(f32).astype(bf16)
    tiles = particles // LANES

    def form(start, tile, on_diagonal):
        at_rows, at_lanes = pl.ds(start, 16), pl.ds(tile * LANES, LANES)
        d = [
            pos_cols[at_rows, pl.ds(a * LANES, LANES)] - pos_rows[pl.ds(a * 16, 16), at_lanes]
            for a in range(3)
        ]
        q = d[0] * d[0] + d[1] * d[1] + d[2] * d[2]
        if on_diagonal:
            row_label = start + lax.broadcasted_iota(jnp.int32, (16, LANES), 0)
            col_label = tile * LANES + lax.broadcasted_iota(jnp.int32, (16, LANES), 1)
            retain = row_label != col_label
            q = jnp.where(retain, q, 4.0)
        u = lax.rsqrt(q)
        r = q * u
        near = r < 2.0
        u2 = u * u
        f = jnp.where(near, 1.0 - 0.28125 * r, u * (0.75 + 0.5 * u2))
        if on_diagonal:
            f = jnp.where(retain, f, 0.0)
        h = u * jnp.where(near, 0.09375, u2 * (0.75 - 1.5 * u2))
        hd = [h * d[a] for a in range(3)]
        for n, (a, b) in enumerate(BLOCKS):
            element = hd[a] * d[b]
            if a == b:
                element = element + f
            mobility[n, at_rows, at_lanes] = element.astype(bf16)

    def rows_of(b):
        return pl.ds(b * samples, samples)

    def lanes_of(span):
        return pl.ds(span[0] * LANES, (span[1] - span[0]) * LANES)

    def fold(x):
        x = x[:samples] + x[samples : 2 * samples] + x[2 * samples :]
        parts = [x[:, start : start + LANES] for start in range(0, x.shape[1], LANES)]
        return functools.reduce(jnp.add, parts)

    def total(x):
        return jnp.sum(x, axis=1, keepdims=True)

    def thrice(x):
        return jnp.concatenate([x, x, x], axis=0)

    def product(pieces, rows_span, lanes_span):
        zero = jnp.zeros_like(pieces[0])
        columns = []
        for a, b in BLOCKS:
            column = [zero, zero, zero]
            column[a], column[b] = pieces[b], pieces[a]
            columns.append(jnp.concatenate(column, axis=0))
        left = jnp.concatenate(columns, axis=1)
        right = jnp.concatenate(
            [mobility[n, lanes_of(rows_span), lanes_of(lanes_span)] for n in range(6)], axis=0
        )
        return jnp.dot(left, right, preferred_element_type=f32)

    def noise_pieces(span):
        return [narrow[rows_of(b), lanes_of(span)] for b in range(3)]

    per_tile = LANES // (2 * per_device)
    half, last = tiles // 2, tiles - 1
    squares = jnp.zeros((samples, LANES), f32)
    own_turned = jnp.transpose(own_ref[...])

    def members(tile):
        return order[tile * per_tile : (tile + 1) * per_tile]

    def receive(tile):
        at = pl.ds(tile * LANES, LANES)
        for code in members(tile):
            if code:
                finished(gathered.at[code], recv_sem.at[code])
            else:
                finished(gathered.at[0, 1], recv_sem.at[0])
        packed = jnp.concatenate(
            [gathered[code].reshape(2 * per_device, LANES) for code in members(tile)], axis=0
        )
        pos_cols[at, :] = jnp.dot(packed, over_lanes, preferred_element_type=f32)
        turned = lax.dot_general(
            turning, packed, (((1,), (1,)), ((), ())), preferred_element_type=f32
        )
        pos_rows[:, at] = turned[fields:]
        noise_full[:, at] = turned[:fields]
        narrow[:, at] = turned[:fields].astype(bf16)
        if tile == 0:
            noise_full[:, pl.ds(0, per_device)] = own_turned[:fields]
        return fold(noise_full[:, at] * noise_full[:, at])

    for code in order[1:]:
        send_later(code)
    for tile in range(tiles):
        if tile == last:
            image[:, lanes_of((0, last))] = product(noise_pieces((0, last)), (0, last), (0, last))
        squares = squares + receive(tile)
        if tile == last:
            for step in range(LANES // 16):
                for other in range(last):
                    form(last * LANES + step * 16, other, False)
                form(last * LANES + step * 16, last, True)
            for step in range(LANES // 16):
                for other in range(last):
                    form(other * LANES + step * 16, last, False)
        else:

            @pl.loop(0, LANES // 16)
            def _(step, tile=tile):
                for other in range(tile + 1):
                    start = pl.multiple_of(tile * LANES + step * 16, 16)
                    form(start, other, other == tile)
                for other in range(tile):
                    start = pl.multiple_of(other * LANES + step * 16, 16)
                    form(start, tile, False)


    squares = total(squares)
    inverse = 1.0 / (squares + 1e-06)
    late = product(noise_pieces((last, tiles)), (last, tiles), (0, tiles))
    at_earlier, at_last = lanes_of((0, last)), lanes_of((last, tiles))
    at_late = product(noise_pieces((0, last)), (0, last), (last, tiles))
    first_image = jnp.concatenate(
        [image[:, at_earlier] + late[:, : last * LANES], at_late + late[:, last * LANES :]],
        axis=1,
    )

    coupled = total(fold(noise_full[...] * first_image))
    alpha_one = (squares + coupled) * inverse
    slope = (coupled - 1e-06) * inverse
    remainder = first_image - thrice(slope) * noise_full[...]
    remainders = fold(remainder * remainder)
    beta_squared = total(remainders) * inverse + 1e-06

    rounded = remainder.astype(bf16)
    cut = half * LANES
    low = [rounded[b * samples : (b + 1) * samples, :cut] for b in range(3)]
    high = [rounded[b * samples : (b + 1) * samples, cut:] for b in range(3)]
    twice = [piece + piece for piece in high]
    both_halves = [jnp.concatenate([x, y], axis=1) for x, y in zip(low, twice)]
    low_image = product(both_halves, (0, tiles), (0, half))
    high_image = product(high, (half, tiles), (half, tiles))
    quadratic = total(
        remainders
        + fold(remainder[:, :cut] * low_image)
        + fold(remainder[:, cut:] * high_image)
    )
    alpha_two = quadratic * inverse / beta_squared
    det_root = jnp.sqrt(alpha_one * alpha_two - beta_squared)
    trace_root = jnp.sqrt(alpha_one + alpha_two + 2.0 * det_root)
    scale = 0.5 / trace_root
    weight = (alpha_one + det_root) * scale
    result = thrice(weight) * noise_full[:, :LANES] + thrice(scale) * remainder[:, :LANES]
    result = jnp.transpose(result)[:per_device]
    for b in range(3):
        out_ref[b] = result[:, b * samples : (b + 1) * samples]

    finished(gathered.at[0, 1], send_sem.at[0])
    for code in range(1, chips):
        finished(gathered.at[code], send_sem.at[code])


def replicated(mesh, positions, thermal_noise):
    rows, cols = mesh.shape["row"], mesh.shape["col"]
    samples, _, per_device = thermal_noise.shape
    particles = rows * cols * per_device
    chips = rows * cols // 2
    f32, bf16 = jnp.float32, jnp.bfloat16
    vmem = pl.BlockSpec(memory_space=pltpu.VMEM)
    anywhere = pl.BlockSpec(memory_space=pl.ANY)
    out = pl.pallas_call(
        functools.partial(replicated_kernel, rows, cols),
        out_shape=jax.ShapeDtypeStruct((3, per_device, samples), f32),
        in_specs=[anywhere, anywhere],
        out_specs=vmem,
        scratch_shapes=[
            pltpu.VMEM((3, per_device, samples), f32),
            pltpu.VMEM((3, per_device), f32),
            pltpu.VMEM((chips, 2, per_device, LANES), bf16),
            pltpu.VMEM((16, LANES), f32),
            pltpu.VMEM((per_device, LANES), f32),
            pltpu.VMEM((3 * samples, particles), f32),
            pltpu.VMEM((particles, 3 * LANES), f32),
            pltpu.VMEM((3 * 16, particles), f32),
            pltpu.VMEM((6, particles, particles), bf16),
            pltpu.VMEM((3 * samples, particles), bf16),
            pltpu.VMEM((3 * samples, particles), f32),
            pltpu.SemaphoreType.DMA((2,)),
            pltpu.SemaphoreType.DMA((chips,)),
            pltpu.SemaphoreType.DMA((chips,)),
            pltpu.SemaphoreType.REGULAR((chips,)),
        ],
        compiler_params=pltpu.CompilerParams(collective_id=0, has_side_effects=True),
        name="lanczos",
    )(jnp.transpose(thermal_noise, (1, 2, 0)), positions)
    return jnp.transpose(out, (2, 0, 1))


def fits(mesh, positions, thermal_noise):
    rows, cols = mesh.shape["row"], mesh.shape["col"]
    samples, _, particles = thermal_noise.shape
    per_device = particles // (rows * cols)
    return (
        rows & (rows - 1) == 0
        and cols & (cols - 1) == 0
        and min(rows, cols) >= 2
        and 4 * samples == LANES
        and per_device == 16
        and particles % (2 * LANES) == 0
        and 12 * particles * particles <= 2**24
    )


def pair_tensor(rows_pos, cols_pos, retain):
    offsets = [rows_pos[a][None, :] - cols_pos[a][:, None] for a in range(3)]
    squared = offsets[0] * offsets[0] + offsets[1] * offsets[1] + offsets[2] * offsets[2]
    guarded = jnp.where(retain, squared, 4.0)
    inverse = lax.rsqrt(guarded)
    distance = guarded * inverse
    correlation = distance < 2.0
    inverse_cube = inverse * inverse * inverse
    inverse_fifth = inverse_cube * inverse * inverse
    isotropic = jnp.where(
        correlation, 1.0 - 0.28125 * distance, 0.75 * inverse + 0.5 * inverse_cube
    )
    dyadic = jnp.where(correlation, 0.09375 * inverse, 0.75 * inverse_cube - 1.5 * inverse_fifth)
    isotropic = jnp.where(retain, isotropic, 0.0)
    dyadic = jnp.where(retain, dyadic, 0.0)
    columns = []
    for b in range(3):
        elements = []
        for a in range(3):
            element = dyadic * offsets[a] * offsets[b]
            if a == b:
                element = element + isotropic
            elements.append(element)
        columns.append(jnp.stack(elements, axis=1))
    return jnp.stack(columns, axis=0)


def half_image(pos_rows, pos_cols, vec_rows, vec_cols, own_vector):
    row_devices = lax.axis_size("row")
    col_devices = lax.axis_size("col")
    row_index = lax.axis_index("row")
    col_index = lax.axis_index("col")
    samples = own_vector.shape[0]
    per_device = own_vector.shape[2]
    row_count = pos_rows.shape[1]
    row_label = row_index * col_devices * per_device + lax.iota(jnp.int32, row_count)
    group_size = min(row_devices, max(1, 128 // per_device))
    width = group_size * per_device
    group_count = row_devices // group_size
    sum_rows = jnp.zeros((samples, 3, row_count), jnp.float32)
    sum_cols = jnp.zeros((samples, 3, per_device * row_devices), jnp.float32)

    def add_group(group, totals):
        sum_rows, sum_cols = totals
        start = group * width
        cols_pos = lax.dynamic_slice_in_dim(pos_cols, start, width, 1)
        cols_vec = lax.dynamic_slice_in_dim(vec_cols, start, width, 2)
        local_cols = lax.iota(jnp.int32, width)
        segment = group * group_size + local_cols // per_device
        col_label = (segment * col_devices + col_index) * per_device + local_cols % per_device
        keep = segment >= row_index
        upper = (segment != row_index)[:, None] | (row_label[None, :] < col_label[:, None])
        retain = keep[:, None] & upper & (row_label[None, :] != col_label[:, None])
        tensor = pair_tensor(pos_rows, cols_pos, retain).astype(jnp.bfloat16)
        sum_rows = sum_rows + jnp.einsum(
            "kbj,bjai->kai", cols_vec, tensor, preferred_element_type=jnp.float32
        )
        credit = jnp.einsum("kai,bjai->kbj", vec_rows, tensor, preferred_element_type=jnp.float32)
        previous = lax.dynamic_slice_in_dim(sum_cols, start, width, 2)
        sum_cols = lax.dynamic_update_slice_in_dim(sum_cols, previous + credit, start, 2)
        return (sum_rows, sum_cols)

    totals = (sum_rows, sum_cols)
    totals = lax.fori_loop(row_index // group_size, group_count, add_group, totals)
    sum_rows, sum_cols = totals
    mobility_image = own_vector + lax.psum_scatter(sum_rows, "col", scatter_dimension=2, tiled=True)
    return mobility_image + lax.psum_scatter(sum_cols, "row", scatter_dimension=2, tiled=True)


def on_device(positions, thermal_noise):
    squares = lax.psum(jnp.sum(thermal_noise * thermal_noise, axis=(1, 2)), ("row", "col"))
    noise_length = jnp.sqrt(squares + 1e-06)
    basis_one = thermal_noise / noise_length[:, None, None]
    pos_cols, cols_one = (
        lax.all_gather(positions, "row", axis=1, tiled=True),
        lax.all_gather(basis_one, "row", axis=2, tiled=True),
    )
    pos_rows, rows_wide = (
        lax.all_gather(positions, "col", axis=1, tiled=True),
        lax.all_gather(basis_one, "col", axis=2, tiled=True),
    )
    image_one = half_image(
        pos_rows, pos_cols, rows_wide.astype(jnp.bfloat16), cols_one.astype(jnp.bfloat16), basis_one
    )
    alpha_one = lax.psum(jnp.sum(basis_one * image_one, axis=(1, 2)), ("row", "col"))
    remainder = image_one - alpha_one[:, None, None] * basis_one
    beta_squared = lax.psum(jnp.sum(remainder * remainder, axis=(1, 2)), ("row", "col"))
    beta_one = jnp.sqrt(beta_squared + 1e-06)
    basis_two = remainder / beta_one[:, None, None]
    narrow_two = basis_two.astype(jnp.bfloat16)
    cols_two = lax.all_gather(narrow_two, "row", axis=2, tiled=True)
    rows_two = lax.all_gather(narrow_two, "col", axis=2, tiled=True)
    image_two = half_image(pos_rows, pos_cols, rows_two, cols_two, basis_two)
    alpha_two = lax.psum(jnp.sum(basis_two * image_two, axis=(1, 2)), ("row", "col"))
    det_root = jnp.sqrt(alpha_one * alpha_two - beta_one * beta_one)
    trace_root = jnp.sqrt(alpha_one + alpha_two + 2.0 * det_root)
    weight_one = (alpha_one + det_root) / trace_root
    weight_two = beta_one / trace_root
    return (
        0.5
        * noise_length[:, None, None]
        * (weight_one[:, None, None] * basis_one + weight_two[:, None, None] * basis_two)
    )


def solution(mesh):
    specs = dict(
        mesh=mesh,
        in_specs=(P(None, ("row", "col")), P(None, None, ("row", "col"))),
        out_specs=P(None, None, ("row", "col")),
        check_vma=False,
    )

    def program(positions, thermal_noise):
        if fits(mesh, positions, thermal_noise):
            body = functools.partial(replicated, mesh)
        else:
            body = on_device
        return jax.shard_map(body, **specs)(positions, thermal_noise)

    return program
```

```python
import functools

import jax
import jax.numpy as jnp
from jax import lax
from jax.experimental import pallas as pl
from jax.experimental.pallas import tpu as pltpu
from jax.sharding import PartitionSpec as P

LANES = 128
LOGICAL = pl.DeviceIdType.LOGICAL
MUTUAL = 0
BLOCKS = ((0, 0), (1, 1), (2, 2), (0, 1), (0, 2), (1, 2))


def chip_bits(rows, cols):
    bits = [(1, 1)]
    weight = 2
    while weight < rows:
        bits.append((weight * cols, weight // 2))
        weight = 2 * weight
    weight = 2
    while weight < cols:
        bits.append((weight, weight // 2))
        weight = 2 * weight
    return bits


def replicated_kernel(
    rows,
    cols,
    noise_hbm,
    pos_hbm,
    out_ref,
    noise_ref,
    pos_ref,
    gathered,
    stage,
    own_ref,
    noise_full,
    pos_cols,
    pos_rows,
    mobility,
    narrow,
    image,
    load_sem,
    send_sem,
    recv_sem,
    grant,
):
    _, per_device, samples = noise_ref.shape
    particles = rows * cols * per_device
    f32, bf16 = jnp.float32, jnp.bfloat16
    my_row, my_col = lax.axis_index("row"), lax.axis_index("col")

    load_pos = pltpu.make_async_copy(pos_hbm, pos_ref, load_sem.at[0])
    load_noise = pltpu.make_async_copy(noise_hbm, noise_ref, load_sem.at[1])
    load_pos.start()
    load_noise.start()

    bits = chip_bits(rows, cols)
    chips = rows * cols // 2
    me = my_row * cols + my_col
    core = lax.rem(my_row, 2)
    mate = cols * (1 - 2 * core)
    my_code = 0
    device, ahead, level = {0: me}, {0: 0}, {0: 0}
    for index, (weight, height) in enumerate(bits):
        digit = lax.rem(me // weight, 2)
        my_code = my_code + (digit << index)
        sign = 1 - 2 * digit
        for code in range(1 << index):
            device[code + (1 << index)] = device[code] + weight * sign
            ahead[code + (1 << index)] = ahead[code] + height * sign
            level[code + (1 << index)] = level[code] + height
    order = sorted(range(chips), key=lambda code: (level[code], code))

    def both(code):
        return device[code], device[code] + mate

    barrier = pltpu.get_barrier_semaphore()
    pl.semaphore_signal(barrier, inc=1, device_id=me + mate, device_id_type=LOGICAL)
    greetings = 1
    for code in order[1:]:
        greetings = greetings + jnp.where(ahead[code] <= MUTUAL, 2, 0)

        @pl.when(ahead[code] >= -MUTUAL)
        def _(code=code):
            for target in both(code):
                pl.semaphore_signal(barrier, inc=1, device_id=target, device_id_type=LOGICAL)

    stage[...] = jnp.zeros_like(stage)
    own_ref[...] = jnp.zeros_like(own_ref)
    load_pos.wait()
    position = pos_ref[...]
    for term in range(3):
        piece = position.astype(bf16).astype(f32)
        stage[pl.ds(3 * term, 3), pl.ds(0, per_device)] = piece
        position = position - piece
    turned = jnp.transpose(stage[...])
    own_ref[:, pl.ds(3 * samples, 16)] = turned[0:per_device, :]

    pl.semaphore_wait(barrier, greetings)
    for code in order[:0:-1]:

        @pl.when(ahead[code] < -MUTUAL)
        def _(code=code):
            for target in both(code):
                pl.semaphore_signal(
                    grant.at[code], inc=1, device_id=target, device_id_type=LOGICAL
                )

    load_noise.wait()
    for b in range(3):
        own_ref[:, pl.ds(b * samples, samples)] = noise_ref[b]
    gathered[0, 0] = own_ref[...].astype(bf16)

    def send(code, side, target):
        pltpu.make_async_remote_copy(
            src_ref=gathered.at[0, 0],
            dst_ref=gathered.at[code, side],
            send_sem=send_sem.at[code],
            recv_sem=recv_sem.at[code],
            device_id=target,
            device_id_type=LOGICAL,
        ).start()

    def finished(ref, semaphore):
        pltpu.make_async_copy(ref, ref, semaphore).wait()

    @pl.when(my_code > 0)
    def _():
        for side in range(2):
            send(my_code, side, core * cols + side * mate)

    for code in order[:0:-1]:

        @pl.when((ahead[code] <= MUTUAL) & (my_code != code))
        def _(code=code):
            for side, target in enumerate(both(code)):
                send(code, side, target)

    send(0, 1, me + mate)

    def send_later(code):
        @pl.when(ahead[code] > MUTUAL)
        def _():
            pl.semaphore_wait(grant.at[code], 2)
            for side, target in enumerate(both(code)):
                send(code, side, target)

    lane = lax.broadcasted_iota(jnp.int32, (1, LANES), 1)
    field = lax.broadcasted_iota(jnp.int32, (LANES, 3 * LANES), 0) - 3 * samples
    target = lax.broadcasted_iota(jnp.int32, (LANES, 3 * LANES), 1) // LANES
    select = (field == target) | (field == target + 3) | (field == target + 6)
    over_lanes = select.astype(f32).astype(bf16)
    fields = 3 * samples
    field = lax.broadcasted_iota(jnp.int32, (fields + 3 * 16, LANES), 1)
    target = lax.broadcasted_iota(jnp.int32, (fields + 3 * 16, LANES), 0)
    coordinate = (target - fields) // 16
    moved = (field - fields == coordinate) | (field - fields == coordinate + 3)
    moved = moved | (field - fields == coordinate + 6)
    select = ((target < fields) & (field == target)) | ((target >= fields) & moved)
    turning = select.astype(f32).astype(bf16)
    tiles = particles // LANES

    def form(start, tile, on_diagonal):
        at_rows, at_lanes = pl.ds(start, 16), pl.ds(tile * LANES, LANES)
        d = [
            pos_cols[at_rows, pl.ds(a * LANES, LANES)] - pos_rows[pl.ds(a * 16, 16), at_lanes]
            for a in range(3)
        ]
        q = d[0] * d[0] + d[1] * d[1] + d[2] * d[2]
        if on_diagonal:
            row_label = start + lax.broadcasted_iota(jnp.int32, (16, LANES), 0)
            col_label = tile * LANES + lax.broadcasted_iota(jnp.int32, (16, LANES), 1)
            retain = row_label != col_label
            q = jnp.where(retain, q, 4.0)
        u = lax.rsqrt(q)
        r = q * u
        near = r < 2.0
        u2 = u * u
        f = jnp.where(near, 1.0 - 0.28125 * r, u * (0.75 + 0.5 * u2))
        if on_diagonal:
            f = jnp.where(retain, f, 0.0)
        h = u * jnp.where(near, 0.09375, u2 * (0.75 - 1.5 * u2))
        hd = [h * d[a] for a in range(3)]
        for n, (a, b) in enumerate(BLOCKS):
            element = hd[a] * d[b]
            if a == b:
                element = element + f
            mobility[n, at_rows, at_lanes] = element.astype(bf16)

    def rows_of(b):
        return pl.ds(b * samples, samples)

    def lanes_of(span):
        return pl.ds(span[0] * LANES, (span[1] - span[0]) * LANES)

    def fold(x):
        x = x[:samples] + x[samples : 2 * samples] + x[2 * samples :]
        parts = [x[:, start : start + LANES] for start in range(0, x.shape[1], LANES)]
        return functools.reduce(jnp.add, parts)

    def total(x):
        return jnp.sum(x, axis=1, keepdims=True)

    def thrice(x):
        return jnp.concatenate([x, x, x], axis=0)

    def product(pieces, rows_span, lanes_span):
        zero = jnp.zeros_like(pieces[0])
        columns = []
        for a, b in BLOCKS:
            column = [zero, zero, zero]
            column[a], column[b] = pieces[b], pieces[a]
            columns.append(jnp.concatenate(column, axis=0))
        left = jnp.concatenate(columns, axis=1)
        right = jnp.concatenate(
            [mobility[n, lanes_of(rows_span), lanes_of(lanes_span)] for n in range(6)], axis=0
        )
        return jnp.dot(left, right, preferred_element_type=f32)

    def noise_pieces(span):
        return [narrow[rows_of(b), lanes_of(span)] for b in range(3)]

    per_tile = LANES // (2 * per_device)
    half, last = tiles // 2, tiles - 1
    squares = jnp.zeros((samples, LANES), f32)
    own_turned = jnp.transpose(own_ref[...])

    def members(tile):
        return order[tile * per_tile : (tile + 1) * per_tile]

    def receive(tile):
        at = pl.ds(tile * LANES, LANES)
        for code in members(tile):
            if code:
                finished(gathered.at[code], recv_sem.at[code])
            else:
                finished(gathered.at[0, 1], recv_sem.at[0])
        packed = jnp.concatenate(
            [gathered[code].reshape(2 * per_device, LANES) for code in members(tile)], axis=0
        )
        pos_cols[at, :] = jnp.dot(packed, over_lanes, preferred_element_type=f32)
        turned = lax.dot_general(
            turning, packed, (((1,), (1,)), ((), ())), preferred_element_type=f32
        )
        pos_rows[:, at] = turned[fields:]
        noise_full[:, at] = turned[:fields]
        narrow[:, at] = turned[:fields].astype(bf16)
        if tile == 0:
            noise_full[:, pl.ds(0, per_device)] = own_turned[:fields]
        return fold(noise_full[:, at] * noise_full[:, at])

    for code in order[1:]:
        send_later(code)
    for tile in range(tiles):
        if tile == last:
            image[:, lanes_of((0, last))] = product(noise_pieces((0, last)), (0, last), (0, last))
        squares = squares + receive(tile)
        if tile == last:
            for step in range(LANES // 16):
                for other in range(last):
                    form(last * LANES + step * 16, other, False)
                form(last * LANES + step * 16, last, True)
            for step in range(LANES // 16):
                for other in range(last):
                    form(other * LANES + step * 16, last, False)
        else:

            @pl.loop(0, LANES // 16)
            def _(step, tile=tile):
                for other in range(tile + 1):
                    start = pl.multiple_of(tile * LANES + step * 16, 16)
                    form(start, other, other == tile)
                for other in range(tile):
                    start = pl.multiple_of(other * LANES + step * 16, 16)
                    form(start, tile, False)


    squares = total(squares)
    inverse = 1.0 / (squares + 1e-06)
    late = product(noise_pieces((last, tiles)), (last, tiles), (0, tiles))
    at_earlier, at_last = lanes_of((0, last)), lanes_of((last, tiles))
    at_late = product(noise_pieces((0, last)), (0, last), (last, tiles))
    first_image = jnp.concatenate(
        [image[:, at_earlier] + late[:, : last * LANES], at_late + late[:, last * LANES :]],
        axis=1,
    )

    coupled = total(fold(noise_full[...] * first_image))
    alpha_one = (squares + coupled) * inverse
    slope = (coupled - 1e-06) * inverse
    remainder = first_image - thrice(slope) * noise_full[...]
    remainders = fold(remainder * remainder)
    beta_squared = total(remainders) * inverse + 1e-06

    rounded = remainder.astype(bf16)
    cut = half * LANES
    low = [rounded[b * samples : (b + 1) * samples, :cut] for b in range(3)]
    high = [rounded[b * samples : (b + 1) * samples, cut:] for b in range(3)]
    twice = [piece + piece for piece in high]
    both_halves = [jnp.concatenate([x, y], axis=1) for x, y in zip(low, twice)]
    low_image = product(both_halves, (0, tiles), (0, half))
    high_image = product(high, (half, tiles), (half, tiles))
    quadratic = total(
        remainders
        + fold(remainder[:, :cut] * low_image)
        + fold(remainder[:, cut:] * high_image)
    )
    alpha_two = quadratic * inverse / beta_squared
    det_root = jnp.sqrt(alpha_one * alpha_two - beta_squared)
    trace_root = jnp.sqrt(alpha_one + alpha_two + 2.0 * det_root)
    scale = 0.5 / trace_root
    weight = (alpha_one + det_root) * scale
    result = thrice(weight) * noise_full[:, :LANES] + thrice(scale) * remainder[:, :LANES]
    result = jnp.transpose(result)[:per_device]
    for b in range(3):
        out_ref[b] = result[:, b * samples : (b + 1) * samples]

    finished(gathered.at[0, 1], send_sem.at[0])
    for code in range(1, chips):
        finished(gathered.at[code], send_sem.at[code])


def replicated(mesh, positions, thermal_noise):
    rows, cols = mesh.shape["row"], mesh.shape["col"]
    samples, _, per_device = thermal_noise.shape
    particles = rows * cols * per_device
    chips = rows * cols // 2
    f32, bf16 = jnp.float32, jnp.bfloat16
    vmem = pl.BlockSpec(memory_space=pltpu.VMEM)
    anywhere = pl.BlockSpec(memory_space=pl.ANY)
    out = pl.pallas_call(
        functools.partial(replicated_kernel, rows, cols),
        out_shape=pltpu.VMEM((3, per_device, samples), f32),
        in_specs=[anywhere, anywhere],
        out_specs=vmem,
        scratch_shapes=[
            pltpu.VMEM((3, per_device, samples), f32),
            pltpu.VMEM((3, per_device), f32),
            pltpu.VMEM((chips, 2, per_device, LANES), bf16),
            pltpu.VMEM((16, LANES), f32),
            pltpu.VMEM((per_device, LANES), f32),
            pltpu.VMEM((3 * samples, particles), f32),
            pltpu.VMEM((particles, 3 * LANES), f32),
            pltpu.VMEM((3 * 16, particles), f32),
            pltpu.VMEM((6, particles, particles), bf16),
            pltpu.VMEM((3 * samples, particles), bf16),
            pltpu.VMEM((3 * samples, particles), f32),
            pltpu.SemaphoreType.DMA((2,)),
            pltpu.SemaphoreType.DMA((chips,)),
            pltpu.SemaphoreType.DMA((chips,)),
            pltpu.SemaphoreType.REGULAR((chips,)),
        ],
        compiler_params=pltpu.CompilerParams(collective_id=0, has_side_effects=True),
        name="lanczos",
    )(jnp.transpose(thermal_noise, (1, 2, 0)), positions)
    return jnp.transpose(out, (2, 0, 1))


def fits(mesh, positions, thermal_noise):
    rows, cols = mesh.shape["row"], mesh.shape["col"]
    samples, _, particles = thermal_noise.shape
    per_device = particles // (rows * cols)
    return (
        rows & (rows - 1) == 0
        and cols & (cols - 1) == 0
        and min(rows, cols) >= 2
        and 4 * samples == LANES
        and per_device == 16
        and particles % (2 * LANES) == 0
        and 12 * particles * particles <= 2**24
    )


def pair_tensor(rows_pos, cols_pos, retain):
    offsets = [rows_pos[a][None, :] - cols_pos[a][:, None] for a in range(3)]
    squared = offsets[0] * offsets[0] + offsets[1] * offsets[1] + offsets[2] * offsets[2]
    guarded = jnp.where(retain, squared, 4.0)
    inverse = lax.rsqrt(guarded)
    distance = guarded * inverse
    correlation = distance < 2.0
    inverse_cube = inverse * inverse * inverse
    inverse_fifth = inverse_cube * inverse * inverse
    isotropic = jnp.where(
        correlation, 1.0 - 0.28125 * distance, 0.75 * inverse + 0.5 * inverse_cube
    )
    dyadic = jnp.where(correlation, 0.09375 * inverse, 0.75 * inverse_cube - 1.5 * inverse_fifth)
    isotropic = jnp.where(retain, isotropic, 0.0)
    dyadic = jnp.where(retain, dyadic, 0.0)
    columns = []
    for b in range(3):
        elements = []
        for a in range(3):
            element = dyadic * offsets[a] * offsets[b]
            if a == b:
                element = element + isotropic
            elements.append(element)
        columns.append(jnp.stack(elements, axis=1))
    return jnp.stack(columns, axis=0)


def half_image(pos_rows, pos_cols, vec_rows, vec_cols, own_vector):
    row_devices = lax.axis_size("row")
    col_devices = lax.axis_size("col")
    row_index = lax.axis_index("row")
    col_index = lax.axis_index("col")
    samples = own_vector.shape[0]
    per_device = own_vector.shape[2]
    row_count = pos_rows.shape[1]
    row_label = row_index * col_devices * per_device + lax.iota(jnp.int32, row_count)
    group_size = min(row_devices, max(1, 128 // per_device))
    width = group_size * per_device
    group_count = row_devices // group_size
    sum_rows = jnp.zeros((samples, 3, row_count), jnp.float32)
    sum_cols = jnp.zeros((samples, 3, per_device * row_devices), jnp.float32)

    def add_group(group, totals):
        sum_rows, sum_cols = totals
        start = group * width
        cols_pos = lax.dynamic_slice_in_dim(pos_cols, start, width, 1)
        cols_vec = lax.dynamic_slice_in_dim(vec_cols, start, width, 2)
        local_cols = lax.iota(jnp.int32, width)
        segment = group * group_size + local_cols // per_device
        col_label = (segment * col_devices + col_index) * per_device + local_cols % per_device
        keep = segment >= row_index
        upper = (segment != row_index)[:, None] | (row_label[None, :] < col_label[:, None])
        retain = keep[:, None] & upper & (row_label[None, :] != col_label[:, None])
        tensor = pair_tensor(pos_rows, cols_pos, retain).astype(jnp.bfloat16)
        sum_rows = sum_rows + jnp.einsum(
            "kbj,bjai->kai", cols_vec, tensor, preferred_element_type=jnp.float32
        )
        credit = jnp.einsum("kai,bjai->kbj", vec_rows, tensor, preferred_element_type=jnp.float32)
        previous = lax.dynamic_slice_in_dim(sum_cols, start, width, 2)
        sum_cols = lax.dynamic_update_slice_in_dim(sum_cols, previous + credit, start, 2)
        return (sum_rows, sum_cols)

    totals = (sum_rows, sum_cols)
    totals = lax.fori_loop(row_index // group_size, group_count, add_group, totals)
    sum_rows, sum_cols = totals
    mobility_image = own_vector + lax.psum_scatter(sum_rows, "col", scatter_dimension=2, tiled=True)
    return mobility_image + lax.psum_scatter(sum_cols, "row", scatter_dimension=2, tiled=True)


def on_device(positions, thermal_noise):
    squares = lax.psum(jnp.sum(thermal_noise * thermal_noise, axis=(1, 2)), ("row", "col"))
    noise_length = jnp.sqrt(squares + 1e-06)
    basis_one = thermal_noise / noise_length[:, None, None]
    pos_cols, cols_one = (
        lax.all_gather(positions, "row", axis=1, tiled=True),
        lax.all_gather(basis_one, "row", axis=2, tiled=True),
    )
    pos_rows, rows_wide = (
        lax.all_gather(positions, "col", axis=1, tiled=True),
        lax.all_gather(basis_one, "col", axis=2, tiled=True),
    )
    image_one = half_image(
        pos_rows, pos_cols, rows_wide.astype(jnp.bfloat16), cols_one.astype(jnp.bfloat16), basis_one
    )
    alpha_one = lax.psum(jnp.sum(basis_one * image_one, axis=(1, 2)), ("row", "col"))
    remainder = image_one - alpha_one[:, None, None] * basis_one
    beta_squared = lax.psum(jnp.sum(remainder * remainder, axis=(1, 2)), ("row", "col"))
    beta_one = jnp.sqrt(beta_squared + 1e-06)
    basis_two = remainder / beta_one[:, None, None]
    narrow_two = basis_two.astype(jnp.bfloat16)
    cols_two = lax.all_gather(narrow_two, "row", axis=2, tiled=True)
    rows_two = lax.all_gather(narrow_two, "col", axis=2, tiled=True)
    image_two = half_image(pos_rows, pos_cols, rows_two, cols_two, basis_two)
    alpha_two = lax.psum(jnp.sum(basis_two * image_two, axis=(1, 2)), ("row", "col"))
    det_root = jnp.sqrt(alpha_one * alpha_two - beta_one * beta_one)
    trace_root = jnp.sqrt(alpha_one + alpha_two + 2.0 * det_root)
    weight_one = (alpha_one + det_root) / trace_root
    weight_two = beta_one / trace_root
    return (
        0.5
        * noise_length[:, None, None]
        * (weight_one[:, None, None] * basis_one + weight_two[:, None, None] * basis_two)
    )


def solution(mesh):
    specs = dict(
        mesh=mesh,
        in_specs=(P(None, ("row", "col")), P(None, None, ("row", "col"))),
        out_specs=P(None, None, ("row", "col")),
        check_vma=False,
    )

    def program(positions, thermal_noise):
        if fits(mesh, positions, thermal_noise):
            body = functools.partial(replicated, mesh)
        else:
            body = on_device
        return jax.shard_map(body, **specs)(positions, thermal_noise)

    return program
```

```python
import functools

import jax
import jax.numpy as jnp
from jax import lax
from jax.experimental import pallas as pl
from jax.experimental.pallas import tpu as pltpu
from jax.sharding import PartitionSpec as P

LANES = 128
LOGICAL = pl.DeviceIdType.LOGICAL
MUTUAL = 0
BLOCKS = ((0, 0), (1, 1), (2, 2), (0, 1), (0, 2), (1, 2))


def chip_bits(rows, cols):
    bits = [(1, 1)]
    weight = 2
    while weight < rows:
        bits.append((weight * cols, weight // 2))
        weight = 2 * weight
    weight = 2
    while weight < cols:
        bits.append((weight, weight // 2))
        weight = 2 * weight
    return bits


def replicated_kernel(
    rows,
    cols,
    noise_hbm,
    pos_hbm,
    out_ref,
    noise_ref,
    pos_ref,
    gathered,
    stage,
    own_ref,
    noise_full,
    pos_cols,
    pos_rows,
    mobility,
    narrow,
    image,
    load_sem,
    send_sem,
    recv_sem,
    grant,
):
    _, per_device, samples = noise_ref.shape
    particles = rows * cols * per_device
    f32, bf16 = jnp.float32, jnp.bfloat16
    my_row, my_col = lax.axis_index("row"), lax.axis_index("col")

    load_pos = pltpu.make_async_copy(pos_hbm, pos_ref, load_sem.at[0])
    load_noise = pltpu.make_async_copy(noise_hbm, noise_ref, load_sem.at[1])
    load_pos.start()
    load_noise.start()

    bits = chip_bits(rows, cols)
    chips = rows * cols // 2
    me = my_row * cols + my_col
    core = lax.rem(my_row, 2)
    mate = cols * (1 - 2 * core)
    my_code = 0
    device, ahead, level = {0: me}, {0: 0}, {0: 0}
    for index, (weight, height) in enumerate(bits):
        digit = lax.rem(me // weight, 2)
        my_code = my_code + (digit << index)
        sign = 1 - 2 * digit
        for code in range(1 << index):
            device[code + (1 << index)] = device[code] + weight * sign
            ahead[code + (1 << index)] = ahead[code] + height * sign
            level[code + (1 << index)] = level[code] + height
    order = sorted(range(chips), key=lambda code: (level[code], code))

    def both(code):
        return device[code], device[code] + mate

    barrier = pltpu.get_barrier_semaphore()
    pl.semaphore_signal(barrier, inc=1, device_id=me + mate, device_id_type=LOGICAL)
    greetings = 1
    for code in order[1:]:
        greetings = greetings + jnp.where(ahead[code] <= MUTUAL, 2, 0)

        @pl.when(ahead[code] >= -MUTUAL)
        def _(code=code):
            for target in both(code):
                pl.semaphore_signal(barrier, inc=1, device_id=target, device_id_type=LOGICAL)

    stage[...] = jnp.zeros_like(stage)
    own_ref[...] = jnp.zeros_like(own_ref)
    load_pos.wait()
    position = pos_ref[...]
    for term in range(3):
        piece = position.astype(bf16).astype(f32)
        stage[pl.ds(3 * term, 3), pl.ds(0, per_device)] = piece
        position = position - piece
    turned = jnp.transpose(stage[...])
    own_ref[:, pl.ds(3 * samples, 16)] = turned[0:per_device, :]

    pl.semaphore_wait(barrier, greetings)
    for code in order[:0:-1]:

        @pl.when(ahead[code] < -MUTUAL)
        def _(code=code):
            for target in both(code):
                pl.semaphore_signal(
                    grant.at[code], inc=1, device_id=target, device_id_type=LOGICAL
                )

    load_noise.wait()
    for b in range(3):
        own_ref[:, pl.ds(b * samples, samples)] = noise_ref[b]
    gathered[0, 0] = own_ref[...].astype(bf16)

    def send(code, side, target):
        pltpu.make_async_remote_copy(
            src_ref=gathered.at[0, 0],
            dst_ref=gathered.at[code, side],
            send_sem=send_sem.at[code],
            recv_sem=recv_sem.at[code],
            device_id=target,
            device_id_type=LOGICAL,
        ).start()

    def finished(ref, semaphore):
        pltpu.make_async_copy(ref, ref, semaphore).wait()

    @pl.when(my_code > 0)
    def _():
        for side in range(2):
            send(my_code, side, core * cols + side * mate)

    for code in order[:0:-1]:

        @pl.when((ahead[code] <= MUTUAL) & (my_code != code))
        def _(code=code):
            for side, target in enumerate(both(code)):
                send(code, side, target)

    send(0, 1, me + mate)

    def send_later(code):
        @pl.when(ahead[code] > MUTUAL)
        def _():
            pl.semaphore_wait(grant.at[code], 2)
            for side, target in enumerate(both(code)):
                send(code, side, target)

    lane = lax.broadcasted_iota(jnp.int32, (1, LANES), 1)
    field = lax.broadcasted_iota(jnp.int32, (LANES, 3 * LANES), 0) - 3 * samples
    target = lax.broadcasted_iota(jnp.int32, (LANES, 3 * LANES), 1) // LANES
    select = (field == target) | (field == target + 3) | (field == target + 6)
    over_lanes = select.astype(f32).astype(bf16)
    fields = 3 * samples
    field = lax.broadcasted_iota(jnp.int32, (fields + 3 * 16, LANES), 1)
    target = lax.broadcasted_iota(jnp.int32, (fields + 3 * 16, LANES), 0)
    coordinate = (target - fields) // 16
    moved = (field - fields == coordinate) | (field - fields == coordinate + 3)
    moved = moved | (field - fields == coordinate + 6)
    select = ((target < fields) & (field == target)) | ((target >= fields) & moved)
    turning = select.astype(f32).astype(bf16)
    tiles = particles // LANES

    def form(start, tile, on_diagonal):
        at_rows, at_lanes = pl.ds(start, 16), pl.ds(tile * LANES, LANES)
        d = [
            pos_cols[at_rows, pl.ds(a * LANES, LANES)] - pos_rows[pl.ds(a * 16, 16), at_lanes]
            for a in range(3)
        ]
        q = d[0] * d[0] + d[1] * d[1] + d[2] * d[2]
        if on_diagonal:
            row_label = start + lax.broadcasted_iota(jnp.int32, (16, LANES), 0)
            col_label = tile * LANES + lax.broadcasted_iota(jnp.int32, (16, LANES), 1)
            retain = row_label != col_label
            q = jnp.where(retain, q, 4.0)
        u = lax.rsqrt(q)
        r = q * u
        near = r < 2.0
        u2 = u * u
        f = jnp.where(near, 1.0 - 0.28125 * r, u * (0.75 + 0.5 * u2))
        if on_diagonal:
            f = jnp.where(retain, f, 0.0)
        h = u * jnp.where(near, 0.09375, u2 * (0.75 - 1.5 * u2))
        hd = [h * d[a] for a in range(3)]
        for n, (a, b) in enumerate(BLOCKS):
            element = hd[a] * d[b]
            if a == b:
                element = element + f
            mobility[n, tile, at_rows, :] = element.astype(bf16)

    def rows_of(b):
        return pl.ds(b * samples, samples)

    def lanes_of(span):
        return pl.ds(span[0] * LANES, (span[1] - span[0]) * LANES)

    def fold(x):
        x = x[:samples] + x[samples : 2 * samples] + x[2 * samples :]
        parts = [x[:, start : start + LANES] for start in range(0, x.shape[1], LANES)]
        return functools.reduce(jnp.add, parts)

    def total(x):
        return jnp.sum(x, axis=1, keepdims=True)

    def thrice(x):
        return jnp.concatenate([x, x, x], axis=0)

    def spread(pieces):
        zero = jnp.zeros_like(pieces[0])
        columns = []
        for a, b in BLOCKS:
            column = [zero, zero, zero]
            column[a], column[b] = pieces[b], pieces[a]
            columns.append(jnp.concatenate(column, axis=0))
        return jnp.concatenate(columns, axis=1)

    def onto(pieces, span, tile):
        right = jnp.concatenate([mobility[n, tile, lanes_of(span), :] for n in range(6)], axis=0)
        return jnp.dot(spread(pieces), right, preferred_element_type=f32)

    def back(pieces, other, tile):
        at = lanes_of((other, other + 1))
        right = jnp.concatenate([mobility[n, tile, at, :] for n in range(6)], axis=1)
        return lax.dot_general(
            spread(pieces), right, (((1,), (1,)), ((), ())), preferred_element_type=f32
        )

    def noise_pieces(span):
        return [narrow[rows_of(b), lanes_of(span)] for b in range(3)]

    per_tile = LANES // (2 * per_device)
    own_turned = jnp.transpose(own_ref[...])

    def members(tile):
        return order[tile * per_tile : (tile + 1) * per_tile]

    def receive(tile):
        at = pl.ds(tile * LANES, LANES)
        for code in members(tile):
            if code:
                finished(gathered.at[code], recv_sem.at[code])
            else:
                finished(gathered.at[0, 1], recv_sem.at[0])
        packed = jnp.concatenate(
            [gathered[code].reshape(2 * per_device, LANES) for code in members(tile)], axis=0
        )
        pos_cols[at, :] = jnp.dot(packed, over_lanes, preferred_element_type=f32)
        turned = lax.dot_general(
            turning, packed, (((1,), (1,)), ((), ())), preferred_element_type=f32
        )
        pos_rows[:, at] = turned[fields:]
        noise_full[:, at] = turned[:fields]
        narrow[:, at] = turned[:fields].astype(bf16)
        if tile == 0:
            noise_full[:, pl.ds(0, per_device)] = own_turned[:fields]

    for code in order[1:]:
        send_later(code)
    for tile in range(tiles):
        receive(tile)
        gained = None
        for other in range(tile + 1):
            for step in range(LANES // 16):
                form(other * LANES + step * 16, tile, other == tile)
            part = onto(noise_pieces((other, other + 1)), (other, other + 1), tile)
            gained = part if gained is None else gained + part
            if other < tile:
                at = lanes_of((other, other + 1))
                image[:, at] = image[:, at] + back(noise_pieces((tile, tile + 1)), other, tile)
        image[:, lanes_of((tile, tile + 1))] = gained

    squares = total(fold(noise_full[...] * noise_full[...]))
    inverse = 1.0 / (squares + 1e-06)
    first_image = image[...]
    coupled = total(fold(noise_full[...] * first_image))
    alpha_one = (squares + coupled) * inverse
    slope = (coupled - 1e-06) * inverse
    remainder = first_image - thrice(slope) * noise_full[...]
    remainders = fold(remainder * remainder)
    beta_squared = total(remainders) * inverse + 1e-06

    rounded = remainder.astype(bf16)
    twice = rounded + rounded
    parts = remainders
    for tile in range(tiles):
        at = slice(tile * LANES, (tile + 1) * LANES)
        pieces = []
        for b in range(3):
            rows_at = slice(b * samples, (b + 1) * samples)
            piece = rounded[rows_at, at]
            if tile:
                piece = jnp.concatenate([twice[rows_at, : tile * LANES], piece], axis=1)
            pieces.append(piece)
        parts = parts + fold(remainder[:, at] * onto(pieces, (0, tile + 1), tile))
    quadratic = total(parts)
    alpha_two = quadratic * inverse / beta_squared
    det_root = jnp.sqrt(alpha_one * alpha_two - beta_squared)
    trace_root = jnp.sqrt(alpha_one + alpha_two + 2.0 * det_root)
    scale = 0.5 / trace_root
    weight = (alpha_one + det_root) * scale
    result = thrice(weight) * noise_full[:, :LANES] + thrice(scale) * remainder[:, :LANES]
    result = jnp.transpose(result)[:per_device]
    for b in range(3):
        out_ref[b] = result[:, b * samples : (b + 1) * samples]

    finished(gathered.at[0, 1], send_sem.at[0])
    for code in range(1, chips):
        finished(gathered.at[code], send_sem.at[code])


def replicated(mesh, positions, thermal_noise):
    rows, cols = mesh.shape["row"], mesh.shape["col"]
    samples, _, per_device = thermal_noise.shape
    particles = rows * cols * per_device
    chips = rows * cols // 2
    f32, bf16 = jnp.float32, jnp.bfloat16
    vmem = pl.BlockSpec(memory_space=pltpu.VMEM)
    anywhere = pl.BlockSpec(memory_space=pl.ANY)
    out = pl.pallas_call(
        functools.partial(replicated_kernel, rows, cols),
        out_shape=pltpu.VMEM((3, per_device, samples), f32),
        in_specs=[anywhere, anywhere],
        out_specs=vmem,
        scratch_shapes=[
            pltpu.VMEM((3, per_device, samples), f32),
            pltpu.VMEM((3, per_device), f32),
            pltpu.VMEM((chips, 2, per_device, LANES), bf16),
            pltpu.VMEM((16, LANES), f32),
            pltpu.VMEM((per_device, LANES), f32),
            pltpu.VMEM((3 * samples, particles), f32),
            pltpu.VMEM((particles, 3 * LANES), f32),
            pltpu.VMEM((3 * 16, particles), f32),
            pltpu.VMEM((6, particles // LANES, particles, LANES), bf16),
            pltpu.VMEM((3 * samples, particles), bf16),
            pltpu.VMEM((3 * samples, particles), f32),
            pltpu.SemaphoreType.DMA((2,)),
            pltpu.SemaphoreType.DMA((chips,)),
            pltpu.SemaphoreType.DMA((chips,)),
            pltpu.SemaphoreType.REGULAR((chips,)),
        ],
        compiler_params=pltpu.CompilerParams(collective_id=0, has_side_effects=True),
        name="lanczos",
    )(jnp.transpose(thermal_noise, (1, 2, 0)), positions)
    return jnp.transpose(out, (2, 0, 1))


def fits(mesh, positions, thermal_noise):
    rows, cols = mesh.shape["row"], mesh.shape["col"]
    samples, _, particles = thermal_noise.shape
    per_device = particles // (rows * cols)
    return (
        rows & (rows - 1) == 0
        and cols & (cols - 1) == 0
        and min(rows, cols) >= 2
        and 4 * samples == LANES
        and per_device == 16
        and particles % (2 * LANES) == 0
        and 12 * particles * particles <= 2**24
    )


def pair_tensor(rows_pos, cols_pos, retain):
    offsets = [rows_pos[a][None, :] - cols_pos[a][:, None] for a in range(3)]
    squared = offsets[0] * offsets[0] + offsets[1] * offsets[1] + offsets[2] * offsets[2]
    guarded = jnp.where(retain, squared, 4.0)
    inverse = lax.rsqrt(guarded)
    distance = guarded * inverse
    correlation = distance < 2.0
    inverse_cube = inverse * inverse * inverse
    inverse_fifth = inverse_cube * inverse * inverse
    isotropic = jnp.where(
        correlation, 1.0 - 0.28125 * distance, 0.75 * inverse + 0.5 * inverse_cube
    )
    dyadic = jnp.where(correlation, 0.09375 * inverse, 0.75 * inverse_cube - 1.5 * inverse_fifth)
    isotropic = jnp.where(retain, isotropic, 0.0)
    dyadic = jnp.where(retain, dyadic, 0.0)
    columns = []
    for b in range(3):
        elements = []
        for a in range(3):
            element = dyadic * offsets[a] * offsets[b]
            if a == b:
                element = element + isotropic
            elements.append(element)
        columns.append(jnp.stack(elements, axis=1))
    return jnp.stack(columns, axis=0)


def half_image(pos_rows, pos_cols, vec_rows, vec_cols, own_vector):
    row_devices = lax.axis_size("row")
    col_devices = lax.axis_size("col")
    row_index = lax.axis_index("row")
    col_index = lax.axis_index("col")
    samples = own_vector.shape[0]
    per_device = own_vector.shape[2]
    row_count = pos_rows.shape[1]
    row_label = row_index * col_devices * per_device + lax.iota(jnp.int32, row_count)
    group_size = min(row_devices, max(1, 128 // per_device))
    width = group_size * per_device
    group_count = row_devices // group_size
    sum_rows = jnp.zeros((samples, 3, row_count), jnp.float32)
    sum_cols = jnp.zeros((samples, 3, per_device * row_devices), jnp.float32)

    def add_group(group, totals):
        sum_rows, sum_cols = totals
        start = group * width
        cols_pos = lax.dynamic_slice_in_dim(pos_cols, start, width, 1)
        cols_vec = lax.dynamic_slice_in_dim(vec_cols, start, width, 2)
        local_cols = lax.iota(jnp.int32, width)
        segment = group * group_size + local_cols // per_device
        col_label = (segment * col_devices + col_index) * per_device + local_cols % per_device
        keep = segment >= row_index
        upper = (segment != row_index)[:, None] | (row_label[None, :] < col_label[:, None])
        retain = keep[:, None] & upper & (row_label[None, :] != col_label[:, None])
        tensor = pair_tensor(pos_rows, cols_pos, retain).astype(jnp.bfloat16)
        sum_rows = sum_rows + jnp.einsum(
            "kbj,bjai->kai", cols_vec, tensor, preferred_element_type=jnp.float32
        )
        credit = jnp.einsum("kai,bjai->kbj", vec_rows, tensor, preferred_element_type=jnp.float32)
        previous = lax.dynamic_slice_in_dim(sum_cols, start, width, 2)
        sum_cols = lax.dynamic_update_slice_in_dim(sum_cols, previous + credit, start, 2)
        return (sum_rows, sum_cols)

    totals = (sum_rows, sum_cols)
    totals = lax.fori_loop(row_index // group_size, group_count, add_group, totals)
    sum_rows, sum_cols = totals
    mobility_image = own_vector + lax.psum_scatter(sum_rows, "col", scatter_dimension=2, tiled=True)
    return mobility_image + lax.psum_scatter(sum_cols, "row", scatter_dimension=2, tiled=True)


def on_device(positions, thermal_noise):
    squares = lax.psum(jnp.sum(thermal_noise * thermal_noise, axis=(1, 2)), ("row", "col"))
    noise_length = jnp.sqrt(squares + 1e-06)
    basis_one = thermal_noise / noise_length[:, None, None]
    pos_cols, cols_one = (
        lax.all_gather(positions, "row", axis=1, tiled=True),
        lax.all_gather(basis_one, "row", axis=2, tiled=True),
    )
    pos_rows, rows_wide = (
        lax.all_gather(positions, "col", axis=1, tiled=True),
        lax.all_gather(basis_one, "col", axis=2, tiled=True),
    )
    image_one = half_image(
        pos_rows, pos_cols, rows_wide.astype(jnp.bfloat16), cols_one.astype(jnp.bfloat16), basis_one
    )
    alpha_one = lax.psum(jnp.sum(basis_one * image_one, axis=(1, 2)), ("row", "col"))
    remainder = image_one - alpha_one[:, None, None] * basis_one
    beta_squared = lax.psum(jnp.sum(remainder * remainder, axis=(1, 2)), ("row", "col"))
    beta_one = jnp.sqrt(beta_squared + 1e-06)
    basis_two = remainder / beta_one[:, None, None]
    narrow_two = basis_two.astype(jnp.bfloat16)
    cols_two = lax.all_gather(narrow_two, "row", axis=2, tiled=True)
    rows_two = lax.all_gather(narrow_two, "col", axis=2, tiled=True)
    image_two = half_image(pos_rows, pos_cols, rows_two, cols_two, basis_two)
    alpha_two = lax.psum(jnp.sum(basis_two * image_two, axis=(1, 2)), ("row", "col"))
    det_root = jnp.sqrt(alpha_one * alpha_two - beta_one * beta_one)
    trace_root = jnp.sqrt(alpha_one + alpha_two + 2.0 * det_root)
    weight_one = (alpha_one + det_root) / trace_root
    weight_two = beta_one / trace_root
    return (
        0.5
        * noise_length[:, None, None]
        * (weight_one[:, None, None] * basis_one + weight_two[:, None, None] * basis_two)
    )


def solution(mesh):
    specs = dict(
        mesh=mesh,
        in_specs=(P(None, ("row", "col")), P(None, None, ("row", "col"))),
        out_specs=P(None, None, ("row", "col")),
        check_vma=False,
    )

    def program(positions, thermal_noise):
        if fits(mesh, positions, thermal_noise):
            body = functools.partial(replicated, mesh)
        else:
            body = on_device
        return jax.shard_map(body, **specs)(positions, thermal_noise)

    return program
```

```python
import functools

import jax
import jax.numpy as jnp
from jax import lax
from jax.experimental import pallas as pl
from jax.experimental.pallas import tpu as pltpu
from jax.sharding import PartitionSpec as P

LANES = 128
LOGICAL = pl.DeviceIdType.LOGICAL
MUTUAL = 0
BLOCKS = ((0, 0), (1, 1), (2, 2), (0, 1), (0, 2), (1, 2))


def chip_bits(rows, cols):
    bits = [(1, 1)]
    weight = 2
    while weight < rows:
        bits.append((weight * cols, weight // 2))
        weight = 2 * weight
    weight = 2
    while weight < cols:
        bits.append((weight, weight // 2))
        weight = 2 * weight
    return bits


def replicated_kernel(
    rows,
    cols,
    noise_hbm,
    pos_hbm,
    out_ref,
    noise_ref,
    pos_ref,
    gathered,
    stage,
    own_ref,
    noise_full,
    pos_cols,
    pos_rows,
    mobility,
    narrow,
    image,
    load_sem,
    send_sem,
    recv_sem,
    grant,
):
    _, per_device, samples = noise_ref.shape
    particles = rows * cols * per_device
    f32, bf16 = jnp.float32, jnp.bfloat16
    my_row, my_col = lax.axis_index("row"), lax.axis_index("col")

    load_pos = pltpu.make_async_copy(pos_hbm, pos_ref, load_sem.at[0])
    load_noise = pltpu.make_async_copy(noise_hbm, noise_ref, load_sem.at[1])
    load_pos.start()
    load_noise.start()

    bits = chip_bits(rows, cols)
    chips = rows * cols // 2
    me = my_row * cols + my_col
    core = lax.rem(my_row, 2)
    mate = cols * (1 - 2 * core)
    my_code = 0
    device, ahead, level = {0: me}, {0: 0}, {0: 0}
    for index, (weight, height) in enumerate(bits):
        digit = lax.rem(me // weight, 2)
        my_code = my_code + (digit << index)
        sign = 1 - 2 * digit
        for code in range(1 << index):
            device[code + (1 << index)] = device[code] + weight * sign
            ahead[code + (1 << index)] = ahead[code] + height * sign
            level[code + (1 << index)] = level[code] + height
    order = sorted(range(chips), key=lambda code: (level[code], code))
    place = {code: index for index, code in enumerate(order)}
    my_place = 0
    for code in order[1:]:
        my_place = my_place + jnp.where(my_code == code, place[code], 0)
    per_tile = LANES // (2 * per_device)

    def both(code):
        return device[code], device[code] + mate

    barrier = pltpu.get_barrier_semaphore()
    pl.semaphore_signal(barrier, inc=1, device_id=me + mate, device_id_type=LOGICAL)
    greetings = 1
    for code in order[1:]:
        greetings = greetings + jnp.where(ahead[code] <= MUTUAL, 2, 0)

        @pl.when(ahead[code] >= -MUTUAL)
        def _(code=code):
            for target in both(code):
                pl.semaphore_signal(barrier, inc=1, device_id=target, device_id_type=LOGICAL)

    stage[...] = jnp.zeros_like(stage)
    own_ref[...] = jnp.zeros_like(own_ref)
    load_pos.wait()
    position = pos_ref[...]
    for term in range(3):
        piece = position.astype(bf16).astype(f32)
        stage[pl.ds(3 * term, 3), pl.ds(0, per_device)] = piece
        position = position - piece
    turned = jnp.transpose(stage[...])
    own_ref[:, pl.ds(3 * samples, 16)] = turned[0:per_device, :]

    load_noise.wait()
    for b in range(3):
        own_ref[:, pl.ds(b * samples, samples)] = noise_ref[b]
    gathered[0] = own_ref[...].astype(bf16)

    pl.semaphore_wait(barrier, greetings)

    def send(spot, side, target):
        pltpu.make_async_remote_copy(
            src_ref=gathered.at[0],
            dst_ref=gathered.at[2 * spot + side],
            send_sem=send_sem.at[0],
            recv_sem=recv_sem.at[spot // per_tile],
            device_id=target,
            device_id_type=LOGICAL,
        ).start()

    def finished(ref, semaphore):
        pltpu.make_async_copy(ref, ref, semaphore).wait()

    @pl.when(my_code > 0)
    def _():
        for side in range(2):
            send(my_place, side, core * cols + side * mate)

    for code in order[:0:-1]:

        @pl.when(ahead[code] < -MUTUAL)
        def _(code=code):
            for target in both(code):
                pl.semaphore_signal(
                    grant.at[code], inc=1, device_id=target, device_id_type=LOGICAL
                )

    for code in order[:0:-1]:

        @pl.when((ahead[code] <= MUTUAL) & (my_code != code))
        def _(code=code):
            for side, target in enumerate(both(code)):
                send(place[code], side, target)

    send(0, 1, me + mate)

    def send_later(code):
        @pl.when(ahead[code] > MUTUAL)
        def _():
            pl.semaphore_wait(grant.at[code], 2)
            for side, target in enumerate(both(code)):
                send(place[code], side, target)

    lane = lax.broadcasted_iota(jnp.int32, (1, LANES), 1)
    field = lax.broadcasted_iota(jnp.int32, (LANES, 3 * LANES), 0) - 3 * samples
    target = lax.broadcasted_iota(jnp.int32, (LANES, 3 * LANES), 1) // LANES
    select = (field == target) | (field == target + 3) | (field == target + 6)
    over_lanes = select.astype(f32).astype(bf16)
    fields = 3 * samples
    field = lax.broadcasted_iota(jnp.int32, (fields + 3 * 16, LANES), 1)
    target = lax.broadcasted_iota(jnp.int32, (fields + 3 * 16, LANES), 0)
    coordinate = (target - fields) // 16
    moved = (field - fields == coordinate) | (field - fields == coordinate + 3)
    moved = moved | (field - fields == coordinate + 6)
    select = ((target < fields) & (field == target)) | ((target >= fields) & moved)
    turning = select.astype(f32).astype(bf16)
    tiles = particles // LANES

    def form(start, tile, on_diagonal):
        at_rows, at_lanes = pl.ds(start, 16), pl.ds(tile * LANES, LANES)
        d = [
            pos_cols[at_rows, pl.ds(a * LANES, LANES)] - pos_rows[pl.ds(a * 16, 16), at_lanes]
            for a in range(3)
        ]
        q = d[0] * d[0] + d[1] * d[1] + d[2] * d[2]
        if on_diagonal:
            row_label = start + lax.broadcasted_iota(jnp.int32, (16, LANES), 0)
            col_label = tile * LANES + lax.broadcasted_iota(jnp.int32, (16, LANES), 1)
            retain = row_label != col_label
            q = jnp.where(retain, q, 4.0)
        u = lax.rsqrt(q)
        r = q * u
        near = r < 2.0
        u2 = u * u
        f = jnp.where(near, 1.0 - 0.28125 * r, u * (0.75 + 0.5 * u2))
        if on_diagonal:
            f = jnp.where(retain, f, 0.0)
        h = u * jnp.where(near, 0.09375, u2 * (0.75 - 1.5 * u2))
        hd = [h * d[a] for a in range(3)]
        for n, (a, b) in enumerate(BLOCKS):
            element = hd[a] * d[b]
            if a == b:
                element = element + f
            mobility[n, tile, at_rows, :] = element.astype(bf16)

    def rows_of(b):
        return pl.ds(b * samples, samples)

    def lanes_of(span):
        return pl.ds(span[0] * LANES, (span[1] - span[0]) * LANES)

    def fold(x):
        x = x[:samples] + x[samples : 2 * samples] + x[2 * samples :]
        parts = [x[:, start : start + LANES] for start in range(0, x.shape[1], LANES)]
        return functools.reduce(jnp.add, parts)

    def total(x):
        return jnp.sum(x, axis=1, keepdims=True)

    def total_row(x):
        return jnp.sum(jnp.transpose(x), axis=0, keepdims=True)

    def thrice(x):
        return jnp.concatenate([x, x, x], axis=0)

    def spread(pieces):
        zero = jnp.zeros_like(pieces[0])
        columns = []
        for a, b in BLOCKS:
            column = [zero, zero, zero]
            column[a], column[b] = pieces[b], pieces[a]
            columns.append(jnp.concatenate(column, axis=0))
        return jnp.concatenate(columns, axis=1)

    def onto_wide(pieces, span, tile):
        right = jnp.concatenate([mobility[n, tile, lanes_of(span), :] for n in range(6)], axis=0)
        return jnp.dot(spread(pieces), right, preferred_element_type=f32)

    def back(pieces, other, tile):
        at = lanes_of((other, other + 1))
        right = jnp.concatenate([mobility[n, tile, at, :] for n in range(6)], axis=1)
        return lax.dot_general(
            spread(pieces), right, (((1,), (1,)), ((), ())), preferred_element_type=f32
        )

    def blockwise(pieces, dot):
        sums = [None] * 3
        for n, (a, b) in enumerate(BLOCKS):
            if a == b:
                parts = [(a, dot(pieces[a], n))]
            else:
                part = dot(jnp.concatenate([pieces[b], pieces[a]], axis=0), n)
                parts = [(a, part[:samples]), (b, part[samples:])]
            for c, part in parts:
                sums[c] = part if sums[c] is None else sums[c] + part
        return jnp.concatenate(sums, axis=0)

    def onto(pieces, span, tile):
        def dot(left, n):
            right = mobility[n, tile, lanes_of(span), :]
            return jnp.dot(left, right, preferred_element_type=f32)

        return blockwise(pieces, dot)

    def noise_pieces(span):
        return [narrow[rows_of(b), lanes_of(span)] for b in range(3)]

    own_turned = jnp.transpose(own_ref[...])

    def members(tile):
        return order[tile * per_tile : (tile + 1) * per_tile]

    def receive(tile):
        at = pl.ds(tile * LANES, LANES)
        blocks = 2 * per_tile
        first = max(tile * blocks, 1)
        finished(gathered.at[pl.ds(first, (tile + 1) * blocks - first)], recv_sem.at[tile])
        packed = gathered[pl.ds(tile * blocks, blocks)].reshape(LANES, LANES)
        pos_cols[at, :] = jnp.dot(packed, over_lanes, preferred_element_type=f32)
        turned = lax.dot_general(
            turning, packed, (((1,), (1,)), ((), ())), preferred_element_type=f32
        )
        pos_rows[:, at] = turned[fields:]
        noise_full[:, at] = turned[:fields]
        narrow[:, at] = turned[:fields].astype(bf16)
        if tile == 0:
            noise_full[:, pl.ds(0, per_device)] = own_turned[:fields]

    for code in order[1:]:
        send_later(code)
    for tile in range(tiles):
        receive(tile)
        gained = None
        for other in range(tile + 1):
            for step in range(LANES // 16):
                form(other * LANES + step * 16, tile, other == tile)
            part = onto_wide(noise_pieces((other, other + 1)), (other, other + 1), tile)
            gained = part if gained is None else gained + part
            if other < tile:
                at = lanes_of((other, other + 1))
                image[:, at] = image[:, at] + back(noise_pieces((tile, tile + 1)), other, tile)
        image[:, lanes_of((tile, tile + 1))] = gained

    square_parts = fold(noise_full[...] * noise_full[...])
    inverse = 1.0 / (total(square_parts) + 1e-06)
    first_image = image[...]
    coupled_parts = fold(noise_full[...] * first_image)
    slope = (total(coupled_parts) - 1e-06) * inverse
    remainder = first_image - thrice(slope) * noise_full[...]
    remainders = fold(remainder * remainder)

    rounded = remainder.astype(bf16)
    twice = rounded + rounded
    parts = remainders
    for tile in range(tiles):
        at = slice(tile * LANES, (tile + 1) * LANES)
        pieces = []
        for b in range(3):
            rows_at = slice(b * samples, (b + 1) * samples)
            piece = rounded[rows_at, at]
            if tile:
                piece = jnp.concatenate([twice[rows_at, : tile * LANES], piece], axis=1)
            pieces.append(piece)
        parts = parts + fold(remainder[:, at] * onto(pieces, (0, tile + 1), tile))

    squares, coupled = total_row(square_parts), total_row(coupled_parts)
    inverse = 1.0 / (squares + 1e-06)
    alpha_one = (squares + coupled) * inverse
    beta_squared = total_row(remainders) * inverse + 1e-06
    ratio = inverse / beta_squared
    own_remainder = jnp.transpose(remainder[:, :LANES])[:per_device]
    alpha_two = total_row(parts) * ratio
    det_root = jnp.sqrt(alpha_one * alpha_two - beta_squared)
    trace_root = jnp.sqrt(alpha_one + alpha_two + 2.0 * det_root)
    scale = 0.5 / trace_root
    weight = (alpha_one + det_root) * scale
    for b in range(3):
        own = own_remainder[:, b * samples : (b + 1) * samples]
        out_ref[b] = weight * noise_ref[b] + scale * own

    finished(gathered.at[pl.ds(1, 2 * chips - 1)], send_sem.at[0])


def replicated(mesh, positions, thermal_noise):
    rows, cols = mesh.shape["row"], mesh.shape["col"]
    samples, _, per_device = thermal_noise.shape
    particles = rows * cols * per_device
    chips = rows * cols // 2
    f32, bf16 = jnp.float32, jnp.bfloat16
    vmem = pl.BlockSpec(memory_space=pltpu.VMEM)
    anywhere = pl.BlockSpec(memory_space=pl.ANY)
    out = pl.pallas_call(
        functools.partial(replicated_kernel, rows, cols),
        out_shape=pltpu.VMEM((3, per_device, samples), f32),
        in_specs=[anywhere, anywhere],
        out_specs=vmem,
        scratch_shapes=[
            pltpu.VMEM((3, per_device, samples), f32),
            pltpu.VMEM((3, per_device), f32),
            pltpu.VMEM((2 * chips, per_device, LANES), bf16),
            pltpu.VMEM((16, LANES), f32),
            pltpu.VMEM((per_device, LANES), f32),
            pltpu.VMEM((3 * samples, particles), f32),
            pltpu.VMEM((particles, 3 * LANES), f32),
            pltpu.VMEM((3 * 16, particles), f32),
            pltpu.VMEM((6, particles // LANES, particles, LANES), bf16),
            pltpu.VMEM((3 * samples, particles), bf16),
            pltpu.VMEM((3 * samples, particles), f32),
            pltpu.SemaphoreType.DMA((2,)),
            pltpu.SemaphoreType.DMA((1,)),
            pltpu.SemaphoreType.DMA((particles // LANES,)),
            pltpu.SemaphoreType.REGULAR((chips,)),
        ],
        compiler_params=pltpu.CompilerParams(collective_id=0, has_side_effects=True),
        name="lanczos",
    )(jnp.transpose(thermal_noise, (1, 2, 0)), positions)
    return jnp.transpose(out, (2, 0, 1))


def fits(mesh, positions, thermal_noise):
    rows, cols = mesh.shape["row"], mesh.shape["col"]
    samples, _, particles = thermal_noise.shape
    per_device = particles // (rows * cols)
    return (
        rows & (rows - 1) == 0
        and cols & (cols - 1) == 0
        and min(rows, cols) >= 2
        and 4 * samples == LANES
        and per_device == 16
        and particles % (2 * LANES) == 0
        and 12 * particles * particles <= 2**24
    )


def pair_tensor(rows_pos, cols_pos, retain):
    offsets = [rows_pos[a][None, :] - cols_pos[a][:, None] for a in range(3)]
    squared = offsets[0] * offsets[0] + offsets[1] * offsets[1] + offsets[2] * offsets[2]
    guarded = jnp.where(retain, squared, 4.0)
    inverse = lax.rsqrt(guarded)
    distance = guarded * inverse
    correlation = distance < 2.0
    inverse_cube = inverse * inverse * inverse
    inverse_fifth = inverse_cube * inverse * inverse
    isotropic = jnp.where(
        correlation, 1.0 - 0.28125 * distance, 0.75 * inverse + 0.5 * inverse_cube
    )
    dyadic = jnp.where(correlation, 0.09375 * inverse, 0.75 * inverse_cube - 1.5 * inverse_fifth)
    isotropic = jnp.where(retain, isotropic, 0.0)
    dyadic = jnp.where(retain, dyadic, 0.0)
    columns = []
    for b in range(3):
        elements = []
        for a in range(3):
            element = dyadic * offsets[a] * offsets[b]
            if a == b:
                element = element + isotropic
            elements.append(element)
        columns.append(jnp.stack(elements, axis=1))
    return jnp.stack(columns, axis=0)


def half_image(pos_rows, pos_cols, vec_rows, vec_cols, own_vector):
    row_devices = lax.axis_size("row")
    col_devices = lax.axis_size("col")
    row_index = lax.axis_index("row")
    col_index = lax.axis_index("col")
    samples = own_vector.shape[0]
    per_device = own_vector.shape[2]
    row_count = pos_rows.shape[1]
    row_label = row_index * col_devices * per_device + lax.iota(jnp.int32, row_count)
    group_size = min(row_devices, max(1, 128 // per_device))
    width = group_size * per_device
    group_count = row_devices // group_size
    sum_rows = jnp.zeros((samples, 3, row_count), jnp.float32)
    sum_cols = jnp.zeros((samples, 3, per_device * row_devices), jnp.float32)

    def add_group(group, totals):
        sum_rows, sum_cols = totals
        start = group * width
        cols_pos = lax.dynamic_slice_in_dim(pos_cols, start, width, 1)
        cols_vec = lax.dynamic_slice_in_dim(vec_cols, start, width, 2)
        local_cols = lax.iota(jnp.int32, width)
        segment = group * group_size + local_cols // per_device
        col_label = (segment * col_devices + col_index) * per_device + local_cols % per_device
        keep = segment >= row_index
        upper = (segment != row_index)[:, None] | (row_label[None, :] < col_label[:, None])
        retain = keep[:, None] & upper & (row_label[None, :] != col_label[:, None])
        tensor = pair_tensor(pos_rows, cols_pos, retain).astype(jnp.bfloat16)
        sum_rows = sum_rows + jnp.einsum(
            "kbj,bjai->kai", cols_vec, tensor, preferred_element_type=jnp.float32
        )
        credit = jnp.einsum("kai,bjai->kbj", vec_rows, tensor, preferred_element_type=jnp.float32)
        previous = lax.dynamic_slice_in_dim(sum_cols, start, width, 2)
        sum_cols = lax.dynamic_update_slice_in_dim(sum_cols, previous + credit, start, 2)
        return (sum_rows, sum_cols)

    totals = (sum_rows, sum_cols)
    totals = lax.fori_loop(row_index // group_size, group_count, add_group, totals)
    sum_rows, sum_cols = totals
    mobility_image = own_vector + lax.psum_scatter(sum_rows, "col", scatter_dimension=2, tiled=True)
    return mobility_image + lax.psum_scatter(sum_cols, "row", scatter_dimension=2, tiled=True)


def on_device(positions, thermal_noise):
    squares = lax.psum(jnp.sum(thermal_noise * thermal_noise, axis=(1, 2)), ("row", "col"))
    noise_length = jnp.sqrt(squares + 1e-06)
    basis_one = thermal_noise / noise_length[:, None, None]
    pos_cols, cols_one = (
        lax.all_gather(positions, "row", axis=1, tiled=True),
        lax.all_gather(basis_one, "row", axis=2, tiled=True),
    )
    pos_rows, rows_wide = (
        lax.all_gather(positions, "col", axis=1, tiled=True),
        lax.all_gather(basis_one, "col", axis=2, tiled=True),
    )
    image_one = half_image(
        pos_rows, pos_cols, rows_wide.astype(jnp.bfloat16), cols_one.astype(jnp.bfloat16), basis_one
    )
    alpha_one = lax.psum(jnp.sum(basis_one * image_one, axis=(1, 2)), ("row", "col"))
    remainder = image_one - alpha_one[:, None, None] * basis_one
    beta_squared = lax.psum(jnp.sum(remainder * remainder, axis=(1, 2)), ("row", "col"))
    beta_one = jnp.sqrt(beta_squared + 1e-06)
    basis_two = remainder / beta_one[:, None, None]
    narrow_two = basis_two.astype(jnp.bfloat16)
    cols_two = lax.all_gather(narrow_two, "row", axis=2, tiled=True)
    rows_two = lax.all_gather(narrow_two, "col", axis=2, tiled=True)
    image_two = half_image(pos_rows, pos_cols, rows_two, cols_two, basis_two)
    alpha_two = lax.psum(jnp.sum(basis_two * image_two, axis=(1, 2)), ("row", "col"))
    det_root = jnp.sqrt(alpha_one * alpha_two - beta_one * beta_one)
    trace_root = jnp.sqrt(alpha_one + alpha_two + 2.0 * det_root)
    weight_one = (alpha_one + det_root) / trace_root
    weight_two = beta_one / trace_root
    return (
        0.5
        * noise_length[:, None, None]
        * (weight_one[:, None, None] * basis_one + weight_two[:, None, None] * basis_two)
    )


def solution(mesh):
    specs = dict(
        mesh=mesh,
        in_specs=(P(None, ("row", "col")), P(None, None, ("row", "col"))),
        out_specs=P(None, None, ("row", "col")),
        check_vma=False,
    )

    def program(positions, thermal_noise):
        if fits(mesh, positions, thermal_noise):
            body = functools.partial(replicated, mesh)
        else:
            body = on_device
        return jax.shard_map(body, **specs)(positions, thermal_noise)

    return program
```

```python
import functools

import jax
import jax.numpy as jnp
from jax import lax
from jax.experimental import pallas as pl
from jax.experimental.pallas import tpu as pltpu
from jax.sharding import PartitionSpec as P

LANES = 128
LOGICAL = pl.DeviceIdType.LOGICAL
MUTUAL = 0
BLOCKS = ((0, 0), (1, 1), (2, 2), (0, 1), (0, 2), (1, 2))


def chip_bits(rows, cols):
    bits = [(1, 1)]
    weight = 2
    while weight < rows:
        bits.append((weight * cols, weight // 2))
        weight = 2 * weight
    weight = 2
    while weight < cols:
        bits.append((weight, weight // 2))
        weight = 2 * weight
    return bits


def replicated_kernel(
    rows,
    cols,
    noise_hbm,
    pos_hbm,
    out_ref,
    noise_ref,
    pos_ref,
    gathered,
    stage,
    own_ref,
    noise_full,
    pos_cols,
    pos_rows,
    mobility,
    narrow,
    image,
    load_sem,
    send_sem,
    recv_sem,
    grant,
):
    _, per_device, samples = noise_ref.shape
    particles = rows * cols * per_device
    f32, bf16 = jnp.float32, jnp.bfloat16
    my_row, my_col = lax.axis_index("row"), lax.axis_index("col")

    load_pos = pltpu.make_async_copy(pos_hbm, pos_ref, load_sem.at[0])
    load_noise = pltpu.make_async_copy(noise_hbm, noise_ref, load_sem.at[1])
    load_pos.start()
    load_noise.start()

    bits = chip_bits(rows, cols)
    chips = rows * cols // 2
    me = my_row * cols + my_col
    core = lax.rem(my_row, 2)
    mate = cols * (1 - 2 * core)
    my_code = 0
    device, ahead, level = {0: me}, {0: 0}, {0: 0}
    for index, (weight, height) in enumerate(bits):
        scale = 600 if 2 <= weight < cols else 600
        height = height * scale + (1 << index)
        digit = lax.rem(me // weight, 2)
        my_code = my_code + (digit << index)
        sign = 1 - 2 * digit
        for code in range(1 << index):
            device[code + (1 << index)] = device[code] + weight * sign
            ahead[code + (1 << index)] = ahead[code] + height * sign
            level[code + (1 << index)] = level[code] + height
    order = sorted(range(chips), key=lambda code: (level[code], code))
    place = {code: index for index, code in enumerate(order)}
    my_place = 0
    for code in order[1:]:
        my_place = my_place + jnp.where(my_code == code, place[code], 0)
    per_tile = LANES // (2 * per_device)

    def both(code):
        return device[code], device[code] + mate

    barrier = pltpu.get_barrier_semaphore()
    pl.semaphore_signal(barrier, inc=1, device_id=me + mate, device_id_type=LOGICAL)
    greetings = 1
    for code in order[1:]:
        greetings = greetings + jnp.where(ahead[code] <= MUTUAL, 2, 0)

        @pl.when(ahead[code] >= -MUTUAL)
        def _(code=code):
            for target in both(code):
                pl.semaphore_signal(barrier, inc=1, device_id=target, device_id_type=LOGICAL)

    stage[...] = jnp.zeros_like(stage)
    load_pos.wait()
    position = pos_ref[...]
    for term in range(3):
        piece = position.astype(bf16).astype(f32)
        stage[pl.ds(3 * term, 3), pl.ds(0, per_device)] = piece
        position = position - piece
    turned = jnp.transpose(stage[...])

    load_noise.wait()
    tail = jnp.zeros((per_device, LANES - 3 * samples - 16), f32)
    own = [noise_ref[b] for b in range(3)] + [turned[0:per_device, :], tail]
    own = jnp.concatenate(own, axis=1)
    gathered[0] = own.astype(bf16)
    own_ref[...] = own

    pl.semaphore_wait(barrier, greetings)

    def send(spot, side, target):
        pltpu.make_async_remote_copy(
            src_ref=gathered.at[0],
            dst_ref=gathered.at[2 * spot + side],
            send_sem=send_sem.at[0],
            recv_sem=recv_sem.at[spot // per_tile],
            device_id=target,
            device_id_type=LOGICAL,
        ).start()

    def finished(ref, semaphore):
        pltpu.make_async_copy(ref, ref, semaphore).wait()

    @pl.when(my_code > 0)
    def _():
        send(my_place, core, 0)
        send(my_place, 1 - core, cols)

    for code in order[:0:-1]:

        @pl.when(ahead[code] < -MUTUAL)
        def _(code=code):
            for target in both(code):
                pl.semaphore_signal(
                    grant.at[code], inc=1, device_id=target, device_id_type=LOGICAL
                )

    for code in order[:0:-1]:

        @pl.when((ahead[code] <= MUTUAL) & (my_code != code))
        def _(code=code):
            for side, target in enumerate(both(code)):
                send(place[code], side, target)

    send(0, 1, me + mate)

    def send_later(code):
        @pl.when(ahead[code] > MUTUAL)
        def _():
            pl.semaphore_wait(grant.at[code], 2)
            for side, target in enumerate(both(code)):
                send(place[code], side, target)

    lane = lax.broadcasted_iota(jnp.int32, (1, LANES), 1)
    field = lax.broadcasted_iota(jnp.int32, (LANES, 3 * LANES), 0) - 3 * samples
    target = lax.broadcasted_iota(jnp.int32, (LANES, 3 * LANES), 1) // LANES
    select = (field == target) | (field == target + 3) | (field == target + 6)
    over_lanes = select.astype(f32).astype(bf16)
    fields = 3 * samples
    field = lax.broadcasted_iota(jnp.int32, (fields + 3 * 16, LANES), 1)
    target = lax.broadcasted_iota(jnp.int32, (fields + 3 * 16, LANES), 0)
    coordinate = (target - fields) // 16
    moved = (field - fields == coordinate) | (field - fields == coordinate + 3)
    moved = moved | (field - fields == coordinate + 6)
    select = ((target < fields) & (field == target)) | ((target >= fields) & moved)
    turning = select.astype(f32).astype(bf16)
    tiles = particles // LANES

    def form(start, tile, on_diagonal):
        at_rows, at_lanes = pl.ds(start, 16), pl.ds(tile * LANES, LANES)
        d = [
            pos_cols[at_rows, pl.ds(a * LANES, LANES)] - pos_rows[pl.ds(a * 16, 16), at_lanes]
            for a in range(3)
        ]
        q = d[0] * d[0] + d[1] * d[1] + d[2] * d[2]
        if on_diagonal:
            row_label = start + lax.broadcasted_iota(jnp.int32, (16, LANES), 0)
            col_label = tile * LANES + lax.broadcasted_iota(jnp.int32, (16, LANES), 1)
            retain = row_label != col_label
            q = jnp.where(retain, q, 4.0)
        u = lax.rsqrt(q)
        r = q * u
        near = r < 2.0
        u2 = u * u
        f = jnp.where(near, 1.0 - 0.28125 * r, u * (0.75 + 0.5 * u2))
        if on_diagonal:
            f = jnp.where(retain, f, 0.0)
        h = u * jnp.where(near, 0.09375, u2 * (0.75 - 1.5 * u2))
        hd = [h * d[a] for a in range(3)]
        for n, (a, b) in enumerate(BLOCKS):
            element = hd[a] * d[b]
            if a == b:
                element = element + f
            mobility[n, tile, at_rows, :] = element.astype(bf16)

    def rows_of(b):
        return pl.ds(b * samples, samples)

    def lanes_of(span):
        return pl.ds(span[0] * LANES, (span[1] - span[0]) * LANES)

    def fold(x):
        x = x[:samples] + x[samples : 2 * samples] + x[2 * samples :]
        parts = [x[:, start : start + LANES] for start in range(0, x.shape[1], LANES)]
        return functools.reduce(jnp.add, parts)

    def total(x):
        return jnp.sum(x, axis=1, keepdims=True)

    def total_row(x):
        return jnp.sum(jnp.transpose(x), axis=0, keepdims=True)

    def thrice(x):
        return jnp.concatenate([x, x, x], axis=0)

    def spread(pieces):
        zero = jnp.zeros_like(pieces[0])
        columns = []
        for a, b in BLOCKS:
            column = [zero, zero, zero]
            column[a], column[b] = pieces[b], pieces[a]
            columns.append(jnp.concatenate(column, axis=0))
        return jnp.concatenate(columns, axis=1)

    def onto_wide(pieces, span, tile):
        right = jnp.concatenate([mobility[n, tile, lanes_of(span), :] for n in range(6)], axis=0)
        return jnp.dot(spread(pieces), right, preferred_element_type=f32)

    def back(pieces, other, tile):
        at = lanes_of((other, other + 1))
        right = jnp.concatenate([mobility[n, tile, at, :] for n in range(6)], axis=1)
        return lax.dot_general(
            spread(pieces), right, (((1,), (1,)), ((), ())), preferred_element_type=f32
        )

    def blockwise(pieces, dot):
        sums = [None] * 3
        for n, (a, b) in enumerate(BLOCKS):
            if a == b:
                parts = [(a, dot(pieces[a], n))]
            else:
                part = dot(jnp.concatenate([pieces[b], pieces[a]], axis=0), n)
                parts = [(a, part[:samples]), (b, part[samples:])]
            for c, part in parts:
                sums[c] = part if sums[c] is None else sums[c] + part
        return jnp.concatenate(sums, axis=0)

    def onto(pieces, span, tile):
        def dot(left, n):
            right = mobility[n, tile, lanes_of(span), :]
            return jnp.dot(left, right, preferred_element_type=f32)

        return blockwise(pieces, dot)

    def noise_pieces(span):
        return [narrow[rows_of(b), lanes_of(span)] for b in range(3)]

    own_turned = jnp.transpose(own_ref[...])

    def members(tile):
        return order[tile * per_tile : (tile + 1) * per_tile]

    def receive(tile):
        at = pl.ds(tile * LANES, LANES)
        blocks = 2 * per_tile
        first = max(tile * blocks, 1)
        finished(gathered.at[pl.ds(first, (tile + 1) * blocks - first)], recv_sem.at[tile])
        packed = gathered[pl.ds(tile * blocks, blocks)].reshape(LANES, LANES)
        pos_cols[at, :] = jnp.dot(packed, over_lanes, preferred_element_type=f32)
        turned = lax.dot_general(
            turning, packed, (((1,), (1,)), ((), ())), preferred_element_type=f32
        )
        pos_rows[:, at] = turned[fields:]
        noise_full[:, at] = turned[:fields]
        narrow[:, at] = turned[:fields].astype(bf16)
        if tile == 0:
            noise_full[:, pl.ds(0, per_device)] = own_turned[:fields]

    for code in order[1:]:
        send_later(code)
    for tile in range(tiles):
        receive(tile)
        gained = None
        for other in range(tile + 1):
            for step in range(LANES // 16):
                form(other * LANES + step * 16, tile, other == tile)
            part = onto_wide(noise_pieces((other, other + 1)), (other, other + 1), tile)
            gained = part if gained is None else gained + part
            if other < tile:
                at = lanes_of((other, other + 1))
                image[:, at] = image[:, at] + back(noise_pieces((tile, tile + 1)), other, tile)
        image[:, lanes_of((tile, tile + 1))] = gained

    square_parts = fold(noise_full[...] * noise_full[...])
    inverse = 1.0 / (total(square_parts) + 1e-06)
    first_image = image[...]
    coupled_parts = fold(noise_full[...] * first_image)
    slope = (total(coupled_parts) - 1e-06) * inverse
    remainder = first_image - thrice(slope) * noise_full[...]
    remainders = fold(remainder * remainder)

    rounded = remainder.astype(bf16)
    twice = rounded + rounded
    parts = remainders
    for tile in range(tiles):
        at = slice(tile * LANES, (tile + 1) * LANES)
        pieces = []
        for b in range(3):
            rows_at = slice(b * samples, (b + 1) * samples)
            piece = rounded[rows_at, at]
            if tile:
                piece = jnp.concatenate([twice[rows_at, : tile * LANES], piece], axis=1)
            pieces.append(piece)
        parts = parts + fold(remainder[:, at] * onto(pieces, (0, tile + 1), tile))

    squares, coupled = total_row(square_parts), total_row(coupled_parts)
    inverse = 1.0 / (squares + 1e-06)
    alpha_one = (squares + coupled) * inverse
    beta_squared = total_row(remainders) * inverse + 1e-06
    ratio = inverse / beta_squared
    own_remainder = jnp.transpose(remainder[:, :LANES])[:per_device]
    alpha_two = total_row(parts) * ratio
    det_root = jnp.sqrt(alpha_one * alpha_two - beta_squared)
    trace_root = jnp.sqrt(alpha_one + alpha_two + 2.0 * det_root)
    scale = 0.5 / trace_root
    weight = (alpha_one + det_root) * scale
    for b in range(3):
        own = own_remainder[:, b * samples : (b + 1) * samples]
        out_ref[b] = weight * noise_ref[b] + scale * own

    finished(gathered.at[pl.ds(1, 2 * chips - 1)], send_sem.at[0])


def replicated(mesh, positions, thermal_noise):
    rows, cols = mesh.shape["row"], mesh.shape["col"]
    samples, _, per_device = thermal_noise.shape
    particles = rows * cols * per_device
    chips = rows * cols // 2
    f32, bf16 = jnp.float32, jnp.bfloat16
    vmem = pl.BlockSpec(memory_space=pltpu.VMEM)
    anywhere = pl.BlockSpec(memory_space=pl.ANY)
    out = pl.pallas_call(
        functools.partial(replicated_kernel, rows, cols),
        out_shape=pltpu.VMEM((3, per_device, samples), f32),
        in_specs=[anywhere, anywhere],
        out_specs=vmem,
        scratch_shapes=[
            pltpu.VMEM((3, per_device, samples), f32),
            pltpu.VMEM((3, per_device), f32),
            pltpu.VMEM((2 * chips, per_device, LANES), bf16),
            pltpu.VMEM((16, LANES), f32),
            pltpu.VMEM((per_device, LANES), f32),
            pltpu.VMEM((3 * samples, particles), f32),
            pltpu.VMEM((particles, 3 * LANES), f32),
            pltpu.VMEM((3 * 16, particles), f32),
            pltpu.VMEM((6, particles // LANES, particles, LANES), bf16),
            pltpu.VMEM((3 * samples, particles), bf16),
            pltpu.VMEM((3 * samples, particles), f32),
            pltpu.SemaphoreType.DMA((2,)),
            pltpu.SemaphoreType.DMA((1,)),
            pltpu.SemaphoreType.DMA((particles // LANES,)),
            pltpu.SemaphoreType.REGULAR((chips,)),
        ],
        compiler_params=pltpu.CompilerParams(collective_id=0, has_side_effects=True),
        name="lanczos",
    )(jnp.transpose(thermal_noise, (1, 2, 0)), positions)
    return jnp.transpose(out, (2, 0, 1))


def fits(mesh, positions, thermal_noise):
    rows, cols = mesh.shape["row"], mesh.shape["col"]
    samples, _, particles = thermal_noise.shape
    per_device = particles // (rows * cols)
    return (
        rows & (rows - 1) == 0
        and cols & (cols - 1) == 0
        and min(rows, cols) >= 2
        and 4 * samples == LANES
        and per_device == 16
        and particles % (2 * LANES) == 0
        and 12 * particles * particles <= 2**24
    )


def pair_tensor(rows_pos, cols_pos, retain):
    offsets = [rows_pos[a][None, :] - cols_pos[a][:, None] for a in range(3)]
    squared = offsets[0] * offsets[0] + offsets[1] * offsets[1] + offsets[2] * offsets[2]
    guarded = jnp.where(retain, squared, 4.0)
    inverse = lax.rsqrt(guarded)
    distance = guarded * inverse
    correlation = distance < 2.0
    inverse_cube = inverse * inverse * inverse
    inverse_fifth = inverse_cube * inverse * inverse
    isotropic = jnp.where(
        correlation, 1.0 - 0.28125 * distance, 0.75 * inverse + 0.5 * inverse_cube
    )
    dyadic = jnp.where(correlation, 0.09375 * inverse, 0.75 * inverse_cube - 1.5 * inverse_fifth)
    isotropic = jnp.where(retain, isotropic, 0.0)
    dyadic = jnp.where(retain, dyadic, 0.0)
    columns = []
    for b in range(3):
        elements = []
        for a in range(3):
            element = dyadic * offsets[a] * offsets[b]
            if a == b:
                element = element + isotropic
            elements.append(element)
        columns.append(jnp.stack(elements, axis=1))
    return jnp.stack(columns, axis=0)


def half_image(pos_rows, pos_cols, vec_rows, vec_cols, own_vector):
    row_devices = lax.axis_size("row")
    col_devices = lax.axis_size("col")
    row_index = lax.axis_index("row")
    col_index = lax.axis_index("col")
    samples = own_vector.shape[0]
    per_device = own_vector.shape[2]
    row_count = pos_rows.shape[1]
    row_label = row_index * col_devices * per_device + lax.iota(jnp.int32, row_count)
    group_size = min(row_devices, max(1, 128 // per_device))
    width = group_size * per_device
    group_count = row_devices // group_size
    sum_rows = jnp.zeros((samples, 3, row_count), jnp.float32)
    sum_cols = jnp.zeros((samples, 3, per_device * row_devices), jnp.float32)

    def add_group(group, totals):
        sum_rows, sum_cols = totals
        start = group * width
        cols_pos = lax.dynamic_slice_in_dim(pos_cols, start, width, 1)
        cols_vec = lax.dynamic_slice_in_dim(vec_cols, start, width, 2)
        local_cols = lax.iota(jnp.int32, width)
        segment = group * group_size + local_cols // per_device
        col_label = (segment * col_devices + col_index) * per_device + local_cols % per_device
        keep = segment >= row_index
        upper = (segment != row_index)[:, None] | (row_label[None, :] < col_label[:, None])
        retain = keep[:, None] & upper & (row_label[None, :] != col_label[:, None])
        tensor = pair_tensor(pos_rows, cols_pos, retain).astype(jnp.bfloat16)
        sum_rows = sum_rows + jnp.einsum(
            "kbj,bjai->kai", cols_vec, tensor, preferred_element_type=jnp.float32
        )
        credit = jnp.einsum("kai,bjai->kbj", vec_rows, tensor, preferred_element_type=jnp.float32)
        previous = lax.dynamic_slice_in_dim(sum_cols, start, width, 2)
        sum_cols = lax.dynamic_update_slice_in_dim(sum_cols, previous + credit, start, 2)
        return (sum_rows, sum_cols)

    totals = (sum_rows, sum_cols)
    totals = lax.fori_loop(row_index // group_size, group_count, add_group, totals)
    sum_rows, sum_cols = totals
    mobility_image = own_vector + lax.psum_scatter(sum_rows, "col", scatter_dimension=2, tiled=True)
    return mobility_image + lax.psum_scatter(sum_cols, "row", scatter_dimension=2, tiled=True)


def on_device(positions, thermal_noise):
    squares = lax.psum(jnp.sum(thermal_noise * thermal_noise, axis=(1, 2)), ("row", "col"))
    noise_length = jnp.sqrt(squares + 1e-06)
    basis_one = thermal_noise / noise_length[:, None, None]
    pos_cols, cols_one = (
        lax.all_gather(positions, "row", axis=1, tiled=True),
        lax.all_gather(basis_one, "row", axis=2, tiled=True),
    )
    pos_rows, rows_wide = (
        lax.all_gather(positions, "col", axis=1, tiled=True),
        lax.all_gather(basis_one, "col", axis=2, tiled=True),
    )
    image_one = half_image(
        pos_rows, pos_cols, rows_wide.astype(jnp.bfloat16), cols_one.astype(jnp.bfloat16), basis_one
    )
    alpha_one = lax.psum(jnp.sum(basis_one * image_one, axis=(1, 2)), ("row", "col"))
    remainder = image_one - alpha_one[:, None, None] * basis_one
    beta_squared = lax.psum(jnp.sum(remainder * remainder, axis=(1, 2)), ("row", "col"))
    beta_one = jnp.sqrt(beta_squared + 1e-06)
    basis_two = remainder / beta_one[:, None, None]
    narrow_two = basis_two.astype(jnp.bfloat16)
    cols_two = lax.all_gather(narrow_two, "row", axis=2, tiled=True)
    rows_two = lax.all_gather(narrow_two, "col", axis=2, tiled=True)
    image_two = half_image(pos_rows, pos_cols, rows_two, cols_two, basis_two)
    alpha_two = lax.psum(jnp.sum(basis_two * image_two, axis=(1, 2)), ("row", "col"))
    det_root = jnp.sqrt(alpha_one * alpha_two - beta_one * beta_one)
    trace_root = jnp.sqrt(alpha_one + alpha_two + 2.0 * det_root)
    weight_one = (alpha_one + det_root) / trace_root
    weight_two = beta_one / trace_root
    return (
        0.5
        * noise_length[:, None, None]
        * (weight_one[:, None, None] * basis_one + weight_two[:, None, None] * basis_two)
    )


def solution(mesh):
    specs = dict(
        mesh=mesh,
        in_specs=(P(None, ("row", "col")), P(None, None, ("row", "col"))),
        out_specs=P(None, None, ("row", "col")),
        check_vma=False,
    )

    def program(positions, thermal_noise):
        if fits(mesh, positions, thermal_noise):
            body = functools.partial(replicated, mesh)
        else:
            body = on_device
        return jax.shard_map(body, **specs)(positions, thermal_noise)

    return program
```

```python
import functools

import jax
import jax.numpy as jnp
from jax import lax
from jax.experimental import pallas as pl
from jax.experimental.pallas import tpu as pltpu
from jax.sharding import PartitionSpec as P

LANES = 128
LOGICAL = pl.DeviceIdType.LOGICAL
BLOCKS = ((0, 0), (1, 1), (2, 2), (0, 1), (0, 2), (1, 2))


def chip_bits(rows, cols):
    bits = [(1, 1)]
    weight = 2
    while weight < rows:
        bits.append((weight * cols, weight // 2))
        weight = 2 * weight
    weight = 2
    while weight < cols:
        bits.append((weight, weight // 2))
        weight = 2 * weight
    return bits


def replicated_kernel(
    rows,
    cols,
    noise_hbm,
    pos_hbm,
    out_ref,
    noise_ref,
    pos_ref,
    gathered,
    stage,
    own_ref,
    noise_full,
    pos_cols,
    pos_rows,
    mobility,
    narrow,
    image,
    load_sem,
    send_sem,
    recv_sem,
    grant,
):
    _, per_device, samples = noise_ref.shape
    particles = rows * cols * per_device
    f32, bf16 = jnp.float32, jnp.bfloat16
    my_row, my_col = lax.axis_index("row"), lax.axis_index("col")

    load_pos = pltpu.make_async_copy(pos_hbm, pos_ref, load_sem.at[0])
    load_noise = pltpu.make_async_copy(noise_hbm, noise_ref, load_sem.at[1])
    load_pos.start()
    load_noise.start()

    bits = chip_bits(rows, cols)
    chips = rows * cols // 2
    me = my_row * cols + my_col
    core = lax.rem(my_row, 2)
    mate = cols * (1 - 2 * core)
    my_code = 0
    device, ahead, level = {0: me}, {0: 0}, {0: 0}
    for index, (weight, height) in enumerate(bits):
        step = 18 if 2 <= weight < cols else 20
        height = height * step * chips + (1 << index)
        digit = lax.rem(me // weight, 2)
        my_code = my_code + (digit << index)
        sign = 1 - 2 * digit
        for code in range(1 << index):
            device[code + (1 << index)] = device[code] + weight * sign
            ahead[code + (1 << index)] = ahead[code] + height * sign
            level[code + (1 << index)] = level[code] + height
    order = sorted(range(chips), key=lambda code: (level[code], code))
    place = {code: index for index, code in enumerate(order)}
    my_place = 0
    for code in order[1:]:
        my_place = my_place + jnp.where(my_code == code, place[code], 0)
    per_tile = LANES // (2 * per_device)

    def both(code):
        return device[code], device[code] + mate

    barrier = pltpu.get_barrier_semaphore()
    pl.semaphore_signal(barrier, inc=1, device_id=me + mate, device_id_type=LOGICAL)
    greetings = 1
    for code in order[1:]:
        greetings = greetings + jnp.where(ahead[code] < 0, 2, 0)

        @pl.when(ahead[code] > 0)
        def _(code=code):
            for target in both(code):
                pl.semaphore_signal(barrier, inc=1, device_id=target, device_id_type=LOGICAL)

    stage[...] = jnp.zeros_like(stage)
    load_pos.wait()
    position = pos_ref[...]
    for term in range(3):
        piece = position.astype(bf16).astype(f32)
        stage[pl.ds(3 * term, 3), pl.ds(0, per_device)] = piece
        position = position - piece
    turned = jnp.transpose(stage[...])

    load_noise.wait()
    tail = jnp.zeros((per_device, LANES - 3 * samples - 16), f32)
    own = [noise_ref[b] for b in range(3)] + [turned[0:per_device, :], tail]
    own = jnp.concatenate(own, axis=1)
    gathered[0] = own.astype(bf16)
    own_ref[...] = own

    pl.semaphore_wait(barrier, greetings)

    def send(spot, side, target):
        pltpu.make_async_remote_copy(
            src_ref=gathered.at[0],
            dst_ref=gathered.at[2 * spot + side],
            send_sem=send_sem.at[0],
            recv_sem=recv_sem.at[spot // per_tile],
            device_id=target,
            device_id_type=LOGICAL,
        ).start()

    def finished(ref, semaphore):
        pltpu.make_async_copy(ref, ref, semaphore).wait()

    @pl.when(my_code > 0)
    def _():
        send(my_place, core, 0)
        send(my_place, 1 - core, cols)

    for code in order[:0:-1]:

        @pl.when(ahead[code] < 0)
        def _(code=code):
            for target in both(code):
                pl.semaphore_signal(
                    grant.at[code], inc=1, device_id=target, device_id_type=LOGICAL
                )

    for code in order[:0:-1]:

        @pl.when((ahead[code] < 0) & (my_code != code))
        def _(code=code):
            for side, target in enumerate(both(code)):
                send(place[code], side, target)

    send(0, 1, me + mate)

    def send_later(code):
        @pl.when(ahead[code] > 0)
        def _():
            pl.semaphore_wait(grant.at[code], 2)
            for side, target in enumerate(both(code)):
                send(place[code], side, target)

    lane = lax.broadcasted_iota(jnp.int32, (1, LANES), 1)
    field = lax.broadcasted_iota(jnp.int32, (LANES, 3 * LANES), 0) - 3 * samples
    target = lax.broadcasted_iota(jnp.int32, (LANES, 3 * LANES), 1) // LANES
    select = (field == target) | (field == target + 3) | (field == target + 6)
    over_lanes = select.astype(f32).astype(bf16)
    fields = 3 * samples
    field = lax.broadcasted_iota(jnp.int32, (fields + 3 * 16, LANES), 1)
    target = lax.broadcasted_iota(jnp.int32, (fields + 3 * 16, LANES), 0)
    coordinate = (target - fields) // 16
    moved = (field - fields == coordinate) | (field - fields == coordinate + 3)
    moved = moved | (field - fields == coordinate + 6)
    select = ((target < fields) & (field == target)) | ((target >= fields) & moved)
    turning = select.astype(f32).astype(bf16)
    tiles = particles // LANES

    def form(start, tile, on_diagonal):
        at_rows, at_lanes = pl.ds(start, 16), pl.ds(tile * LANES, LANES)
        d = [
            pos_cols[at_rows, pl.ds(a * LANES, LANES)] - pos_rows[pl.ds(a * 16, 16), at_lanes]
            for a in range(3)
        ]
        q = d[0] * d[0] + d[1] * d[1] + d[2] * d[2]
        if on_diagonal:
            row_label = start + lax.broadcasted_iota(jnp.int32, (16, LANES), 0)
            col_label = tile * LANES + lax.broadcasted_iota(jnp.int32, (16, LANES), 1)
            retain = row_label != col_label
            q = jnp.where(retain, q, 4.0)
        u = lax.rsqrt(q)
        r = q * u
        near = r < 2.0
        u2 = u * u
        f = jnp.where(near, 1.0 - 0.28125 * r, u * (0.75 + 0.5 * u2))
        if on_diagonal:
            f = jnp.where(retain, f, 0.0)
        h = u * jnp.where(near, 0.09375, u2 * (0.75 - 1.5 * u2))
        hd = [h * d[a] for a in range(3)]
        for n, (a, b) in enumerate(BLOCKS):
            element = hd[a] * d[b]
            if a == b:
                element = element + f
            mobility[n, tile, at_rows, :] = element.astype(bf16)

    def rows_of(b):
        return pl.ds(b * samples, samples)

    def lanes_of(span):
        return pl.ds(span[0] * LANES, (span[1] - span[0]) * LANES)

    def fold(x):
        x = x[:samples] + x[samples : 2 * samples] + x[2 * samples :]
        parts = [x[:, start : start + LANES] for start in range(0, x.shape[1], LANES)]
        return functools.reduce(jnp.add, parts)

    def total(x):
        return jnp.sum(x, axis=1, keepdims=True)

    def total_row(x):
        return jnp.sum(jnp.transpose(x), axis=0, keepdims=True)

    def thrice(x):
        return jnp.concatenate([x, x, x], axis=0)

    def spread(pieces):
        zero = jnp.zeros_like(pieces[0])
        columns = []
        for a, b in BLOCKS:
            column = [zero, zero, zero]
            column[a], column[b] = pieces[b], pieces[a]
            columns.append(jnp.concatenate(column, axis=0))
        return jnp.concatenate(columns, axis=1)

    def onto_wide(pieces, span, tile):
        right = jnp.concatenate([mobility[n, tile, lanes_of(span), :] for n in range(6)], axis=0)
        return jnp.dot(spread(pieces), right, preferred_element_type=f32)

    def back(pieces, other, tile):
        at = lanes_of((other, other + 1))
        right = jnp.concatenate([mobility[n, tile, at, :] for n in range(6)], axis=1)
        return lax.dot_general(
            spread(pieces), right, (((1,), (1,)), ((), ())), preferred_element_type=f32
        )

    def blockwise(pieces, dot):
        sums = [None] * 3
        for n, (a, b) in enumerate(BLOCKS):
            if a == b:
                parts = [(a, dot(pieces[a], n))]
            else:
                part = dot(jnp.concatenate([pieces[b], pieces[a]], axis=0), n)
                parts = [(a, part[:samples]), (b, part[samples:])]
            for c, part in parts:
                sums[c] = part if sums[c] is None else sums[c] + part
        return jnp.concatenate(sums, axis=0)

    def onto(pieces, span, tile):
        def dot(left, n):
            right = mobility[n, tile, lanes_of(span), :]
            return jnp.dot(left, right, preferred_element_type=f32)

        return blockwise(pieces, dot)

    def noise_pieces(span):
        return [narrow[rows_of(b), lanes_of(span)] for b in range(3)]

    own_turned = jnp.transpose(own_ref[...])

    def members(tile):
        return order[tile * per_tile : (tile + 1) * per_tile]

    def receive(tile):
        at = pl.ds(tile * LANES, LANES)
        blocks = 2 * per_tile
        first = max(tile * blocks, 1)
        finished(gathered.at[pl.ds(first, (tile + 1) * blocks - first)], recv_sem.at[tile])
        packed = gathered[pl.ds(tile * blocks, blocks)].reshape(LANES, LANES)
        pos_cols[at, :] = jnp.dot(packed, over_lanes, preferred_element_type=f32)
        turned = lax.dot_general(
            turning, packed, (((1,), (1,)), ((), ())), preferred_element_type=f32
        )
        pos_rows[:, at] = turned[fields:]
        noise_full[:, at] = turned[:fields]
        narrow[:, at] = turned[:fields].astype(bf16)
        if tile == 0:
            noise_full[:, pl.ds(0, per_device)] = own_turned[:fields]

    for code in order[1:]:
        send_later(code)
    def spread_products(tile, others, gained=None):
        for other in others:
            part = onto_wide(noise_pieces((other, other + 1)), (other, other + 1), tile)
            gained = part if gained is None else gained + part
            if other < tile:
                at = lanes_of((other, other + 1))
                image[:, at] = image[:, at] + back(noise_pieces((tile, tile + 1)), other, tile)
        return gained

    held = []
    for tile in range(tiles):
        receive(tile)
        for late in held:
            image[:, lanes_of((late, late + 1))] = spread_products(late, range(late + 1))
        held = []
        gained = None
        for other in range(tile + 1):
            for step in range(LANES // 16):
                form(other * LANES + step * 16, tile, other == tile)
            if tile not in range(tiles - 2, tiles - 1):
                gained = spread_products(tile, [other], gained)
        if tile in range(tiles - 2, tiles - 1):
            held.append(tile)
        else:
            image[:, lanes_of((tile, tile + 1))] = gained

    square_parts = fold(noise_full[...] * noise_full[...])
    inverse = 1.0 / (total(square_parts) + 1e-06)
    first_image = image[...]
    coupled_parts = fold(noise_full[...] * first_image)
    slope = (total(coupled_parts) - 1e-06) * inverse
    remainder = first_image - thrice(slope) * noise_full[...]
    remainders = fold(remainder * remainder)

    rounded = remainder.astype(bf16)
    twice = rounded + rounded
    parts = remainders
    for tile in range(tiles):
        at = slice(tile * LANES, (tile + 1) * LANES)
        pieces = []
        for b in range(3):
            rows_at = slice(b * samples, (b + 1) * samples)
            piece = rounded[rows_at, at]
            if tile:
                piece = jnp.concatenate([twice[rows_at, : tile * LANES], piece], axis=1)
            pieces.append(piece)
        parts = parts + fold(remainder[:, at] * onto(pieces, (0, tile + 1), tile))

    squares, coupled = total_row(square_parts), total_row(coupled_parts)
    inverse = 1.0 / (squares + 1e-06)
    alpha_one = (squares + coupled) * inverse
    beta_squared = total_row(remainders) * inverse + 1e-06
    ratio = inverse / beta_squared
    own_remainder = jnp.transpose(remainder[:, :LANES])[:per_device]
    alpha_two = total_row(parts) * ratio
    det_root = jnp.sqrt(alpha_one * alpha_two - beta_squared)
    trace_root = jnp.sqrt(alpha_one + alpha_two + 2.0 * det_root)
    scale = 0.5 / trace_root
    weight = (alpha_one + det_root) * scale
    for b in range(3):
        own = own_remainder[:, b * samples : (b + 1) * samples]
        out_ref[b] = weight * noise_ref[b] + scale * own

    finished(gathered.at[pl.ds(1, 2 * chips - 1)], send_sem.at[0])


def replicated(mesh, positions, thermal_noise):
    rows, cols = mesh.shape["row"], mesh.shape["col"]
    samples, _, per_device = thermal_noise.shape
    particles = rows * cols * per_device
    chips = rows * cols // 2
    f32, bf16 = jnp.float32, jnp.bfloat16
    vmem = pl.BlockSpec(memory_space=pltpu.VMEM)
    anywhere = pl.BlockSpec(memory_space=pl.ANY)
    out = pl.pallas_call(
        functools.partial(replicated_kernel, rows, cols),
        out_shape=pltpu.VMEM((3, per_device, samples), f32),
        in_specs=[anywhere, anywhere],
        out_specs=vmem,
        scratch_shapes=[
            pltpu.VMEM((3, per_device, samples), f32),
            pltpu.VMEM((3, per_device), f32),
            pltpu.VMEM((2 * chips, per_device, LANES), bf16),
            pltpu.VMEM((16, LANES), f32),
            pltpu.VMEM((per_device, LANES), f32),
            pltpu.VMEM((3 * samples, particles), f32),
            pltpu.VMEM((particles, 3 * LANES), f32),
            pltpu.VMEM((3 * 16, particles), f32),
            pltpu.VMEM((6, particles // LANES, particles, LANES), bf16),
            pltpu.VMEM((3 * samples, particles), bf16),
            pltpu.VMEM((3 * samples, particles), f32),
            pltpu.SemaphoreType.DMA((2,)),
            pltpu.SemaphoreType.DMA((1,)),
            pltpu.SemaphoreType.DMA((particles // LANES,)),
            pltpu.SemaphoreType.REGULAR((chips,)),
        ],
        compiler_params=pltpu.CompilerParams(collective_id=0, has_side_effects=True),
        name="lanczos",
    )(jnp.transpose(thermal_noise, (1, 2, 0)), positions)
    return jnp.transpose(out, (2, 0, 1))


def fits(mesh, positions, thermal_noise):
    rows, cols = mesh.shape["row"], mesh.shape["col"]
    samples, _, particles = thermal_noise.shape
    per_device = particles // (rows * cols)
    return (
        rows & (rows - 1) == 0
        and cols & (cols - 1) == 0
        and min(rows, cols) >= 2
        and 4 * samples == LANES
        and per_device == 16
        and particles % (2 * LANES) == 0
        and 12 * particles * particles <= 2**24
    )


def pair_tensor(rows_pos, cols_pos, retain):
    offsets = [rows_pos[a][None, :] - cols_pos[a][:, None] for a in range(3)]
    squared = offsets[0] * offsets[0] + offsets[1] * offsets[1] + offsets[2] * offsets[2]
    guarded = jnp.where(retain, squared, 4.0)
    inverse = lax.rsqrt(guarded)
    distance = guarded * inverse
    correlation = distance < 2.0
    inverse_cube = inverse * inverse * inverse
    inverse_fifth = inverse_cube * inverse * inverse
    isotropic = jnp.where(
        correlation, 1.0 - 0.28125 * distance, 0.75 * inverse + 0.5 * inverse_cube
    )
    dyadic = jnp.where(correlation, 0.09375 * inverse, 0.75 * inverse_cube - 1.5 * inverse_fifth)
    isotropic = jnp.where(retain, isotropic, 0.0)
    dyadic = jnp.where(retain, dyadic, 0.0)
    columns = []
    for b in range(3):
        elements = []
        for a in range(3):
            element = dyadic * offsets[a] * offsets[b]
            if a == b:
                element = element + isotropic
            elements.append(element)
        columns.append(jnp.stack(elements, axis=1))
    return jnp.stack(columns, axis=0)


def half_image(pos_rows, pos_cols, vec_rows, vec_cols, own_vector):
    row_devices = lax.axis_size("row")
    col_devices = lax.axis_size("col")
    row_index = lax.axis_index("row")
    col_index = lax.axis_index("col")
    samples = own_vector.shape[0]
    per_device = own_vector.shape[2]
    row_count = pos_rows.shape[1]
    row_label = row_index * col_devices * per_device + lax.iota(jnp.int32, row_count)
    group_size = min(row_devices, max(1, 128 // per_device))
    width = group_size * per_device
    group_count = row_devices // group_size
    sum_rows = jnp.zeros((samples, 3, row_count), jnp.float32)
    sum_cols = jnp.zeros((samples, 3, per_device * row_devices), jnp.float32)

    def add_group(group, totals):
        sum_rows, sum_cols = totals
        start = group * width
        cols_pos = lax.dynamic_slice_in_dim(pos_cols, start, width, 1)
        cols_vec = lax.dynamic_slice_in_dim(vec_cols, start, width, 2)
        local_cols = lax.iota(jnp.int32, width)
        segment = group * group_size + local_cols // per_device
        col_label = (segment * col_devices + col_index) * per_device + local_cols % per_device
        keep = segment >= row_index
        upper = (segment != row_index)[:, None] | (row_label[None, :] < col_label[:, None])
        retain = keep[:, None] & upper & (row_label[None, :] != col_label[:, None])
        tensor = pair_tensor(pos_rows, cols_pos, retain).astype(jnp.bfloat16)
        sum_rows = sum_rows + jnp.einsum(
            "kbj,bjai->kai", cols_vec, tensor, preferred_element_type=jnp.float32
        )
        credit = jnp.einsum("kai,bjai->kbj", vec_rows, tensor, preferred_element_type=jnp.float32)
        previous = lax.dynamic_slice_in_dim(sum_cols, start, width, 2)
        sum_cols = lax.dynamic_update_slice_in_dim(sum_cols, previous + credit, start, 2)
        return (sum_rows, sum_cols)

    totals = (sum_rows, sum_cols)
    totals = lax.fori_loop(row_index // group_size, group_count, add_group, totals)
    sum_rows, sum_cols = totals
    mobility_image = own_vector + lax.psum_scatter(sum_rows, "col", scatter_dimension=2, tiled=True)
    return mobility_image + lax.psum_scatter(sum_cols, "row", scatter_dimension=2, tiled=True)


def on_device(positions, thermal_noise):
    squares = lax.psum(jnp.sum(thermal_noise * thermal_noise, axis=(1, 2)), ("row", "col"))
    noise_length = jnp.sqrt(squares + 1e-06)
    basis_one = thermal_noise / noise_length[:, None, None]
    pos_cols, cols_one = (
        lax.all_gather(positions, "row", axis=1, tiled=True),
        lax.all_gather(basis_one, "row", axis=2, tiled=True),
    )
    pos_rows, rows_wide = (
        lax.all_gather(positions, "col", axis=1, tiled=True),
        lax.all_gather(basis_one, "col", axis=2, tiled=True),
    )
    image_one = half_image(
        pos_rows, pos_cols, rows_wide.astype(jnp.bfloat16), cols_one.astype(jnp.bfloat16), basis_one
    )
    alpha_one = lax.psum(jnp.sum(basis_one * image_one, axis=(1, 2)), ("row", "col"))
    remainder = image_one - alpha_one[:, None, None] * basis_one
    beta_squared = lax.psum(jnp.sum(remainder * remainder, axis=(1, 2)), ("row", "col"))
    beta_one = jnp.sqrt(beta_squared + 1e-06)
    basis_two = remainder / beta_one[:, None, None]
    narrow_two = basis_two.astype(jnp.bfloat16)
    cols_two = lax.all_gather(narrow_two, "row", axis=2, tiled=True)
    rows_two = lax.all_gather(narrow_two, "col", axis=2, tiled=True)
    image_two = half_image(pos_rows, pos_cols, rows_two, cols_two, basis_two)
    alpha_two = lax.psum(jnp.sum(basis_two * image_two, axis=(1, 2)), ("row", "col"))
    det_root = jnp.sqrt(alpha_one * alpha_two - beta_one * beta_one)
    trace_root = jnp.sqrt(alpha_one + alpha_two + 2.0 * det_root)
    weight_one = (alpha_one + det_root) / trace_root
    weight_two = beta_one / trace_root
    return (
        0.5
        * noise_length[:, None, None]
        * (weight_one[:, None, None] * basis_one + weight_two[:, None, None] * basis_two)
    )


def solution(mesh):
    specs = dict(
        mesh=mesh,
        in_specs=(P(None, ("row", "col")), P(None, None, ("row", "col"))),
        out_specs=P(None, None, ("row", "col")),
        check_vma=False,
    )

    def program(positions, thermal_noise):
        if fits(mesh, positions, thermal_noise):
            body = functools.partial(replicated, mesh)
        else:
            body = on_device
        return jax.shard_map(body, **specs)(positions, thermal_noise)

    return program
```

```python
import functools

import jax
import jax.numpy as jnp
from jax import lax
from jax.experimental import pallas as pl
from jax.experimental.pallas import tpu as pltpu
from jax.sharding import PartitionSpec as P

LANES = 128
SHARED = 2
LOGICAL = pl.DeviceIdType.LOGICAL
BLOCKS = ((0, 0), (1, 1), (2, 2), (0, 1), (0, 2), (1, 2))


def chip_bits(rows, cols):
    bits = [(1, 1)]
    weight = 2
    while weight < rows:
        bits.append((weight * cols, weight // 2))
        weight = 2 * weight
    weight = 2
    while weight < cols:
        bits.append((weight, weight // 2))
        weight = 2 * weight
    return bits


def replicated_kernel(
    rows,
    cols,
    noise_hbm,
    pos_hbm,
    out_ref,
    noise_ref,
    pos_ref,
    gathered,
    stage,
    own_ref,
    noise_full,
    pos_cols,
    pos_rows,
    mobility,
    narrow,
    image,
    load_sem,
    send_sem,
    recv_sem,
    grant,
):
    _, per_device, samples = noise_ref.shape
    particles = rows * cols * per_device
    f32, bf16 = jnp.float32, jnp.bfloat16
    my_row, my_col = lax.axis_index("row"), lax.axis_index("col")

    load_pos = pltpu.make_async_copy(pos_hbm, pos_ref, load_sem.at[0])
    load_noise = pltpu.make_async_copy(noise_hbm, noise_ref, load_sem.at[1])
    load_pos.start()
    load_noise.start()

    bits = chip_bits(rows, cols)
    chips = rows * cols // 2
    me = my_row * cols + my_col
    core = lax.rem(my_row, 2)
    mate = cols * (1 - 2 * core)
    my_code = 0
    device, ahead, level = {0: me}, {0: 0}, {0: 0}
    for index, (weight, height) in enumerate(bits):
        step = 18 if 2 <= weight < cols else 20
        height = height * step * chips + (1 << index)
        digit = lax.rem(me // weight, 2)
        my_code = my_code + (digit << index)
        sign = 1 - 2 * digit
        for code in range(1 << index):
            device[code + (1 << index)] = device[code] + weight * sign
            ahead[code + (1 << index)] = ahead[code] + height * sign
            level[code + (1 << index)] = level[code] + height
    order = sorted(range(chips), key=lambda code: (level[code], code))
    place = {code: index for index, code in enumerate(order)}
    my_place = 0
    for code in order[1:]:
        my_place = my_place + jnp.where(my_code == code, place[code], 0)
    per_tile = LANES // (2 * per_device)

    def both(code):
        return device[code], device[code] + mate

    barrier = pltpu.get_barrier_semaphore()
    pl.semaphore_signal(barrier, inc=1, device_id=me + mate, device_id_type=LOGICAL)
    greetings = 1
    for code in order[1:]:
        greetings = greetings + jnp.where(ahead[code] < 0, 2, 0)

        @pl.when(ahead[code] > 0)
        def _(code=code):
            for target in both(code):
                pl.semaphore_signal(barrier, inc=1, device_id=target, device_id_type=LOGICAL)

    stage[...] = jnp.zeros_like(stage)
    load_pos.wait()
    position = pos_ref[...]
    for term in range(3):
        piece = position.astype(bf16).astype(f32)
        stage[pl.ds(3 * term, 3), pl.ds(0, per_device)] = piece
        position = position - piece
    turned = jnp.transpose(stage[...])

    load_noise.wait()
    tail = jnp.zeros((per_device, LANES - 3 * samples - 16), f32)
    own = [noise_ref[b] for b in range(3)] + [turned[0:per_device, :], tail]
    own = jnp.concatenate(own, axis=1)
    gathered[0] = own.astype(bf16)
    own_ref[...] = own

    pl.semaphore_wait(barrier, greetings)

    def send(spot, side, target):
        pltpu.make_async_remote_copy(
            src_ref=gathered.at[0],
            dst_ref=gathered.at[2 * spot + side],
            send_sem=send_sem.at[0],
            recv_sem=recv_sem.at[spot // per_tile],
            device_id=target,
            device_id_type=LOGICAL,
        ).start()

    def finished(ref, semaphore):
        pltpu.make_async_copy(ref, ref, semaphore).wait()

    @pl.when(my_code > 0)
    def _():
        send(my_place, core, 0)
        send(my_place, 1 - core, cols)

    for code in order[:0:-1]:

        @pl.when(ahead[code] < 0)
        def _(code=code):
            for target in both(code):
                pl.semaphore_signal(
                    grant.at[place[code] // SHARED], inc=1, device_id=target, device_id_type=LOGICAL
                )

    for code in order[:0:-1]:

        @pl.when((ahead[code] < 0) & (my_code != code))
        def _(code=code):
            for side, target in enumerate(both(code)):
                send(place[code], side, target)

    send(0, 1, me + mate)

    def send_later(group):
        codes = [code for code in order[group * SHARED : (group + 1) * SHARED] if code]
        owed = 0
        for code in codes:
            owed = owed + jnp.where(ahead[code] > 0, 2, 0)

        @pl.when(owed > 0)
        def _():
            pl.semaphore_wait(grant.at[group], owed)
            for code in codes:

                @pl.when(ahead[code] > 0)
                def _(code=code):
                    for side, target in enumerate(both(code)):
                        send(place[code], side, target)

    lane = lax.broadcasted_iota(jnp.int32, (1, LANES), 1)
    field = lax.broadcasted_iota(jnp.int32, (LANES, 3 * LANES), 0) - 3 * samples
    target = lax.broadcasted_iota(jnp.int32, (LANES, 3 * LANES), 1) // LANES
    select = (field == target) | (field == target + 3) | (field == target + 6)
    over_lanes = select.astype(f32).astype(bf16)
    fields = 3 * samples
    field = lax.broadcasted_iota(jnp.int32, (fields + 3 * 16, LANES), 1)
    target = lax.broadcasted_iota(jnp.int32, (fields + 3 * 16, LANES), 0)
    coordinate = (target - fields) // 16
    moved = (field - fields == coordinate) | (field - fields == coordinate + 3)
    moved = moved | (field - fields == coordinate + 6)
    select = ((target < fields) & (field == target)) | ((target >= fields) & moved)
    turning = select.astype(f32).astype(bf16)
    tiles = particles // LANES

    def form(start, tile, on_diagonal):
        at_rows, at_lanes = pl.ds(start, 16), pl.ds(tile * LANES, LANES)
        d = [
            pos_cols[at_rows, pl.ds(a * LANES, LANES)] - pos_rows[pl.ds(a * 16, 16), at_lanes]
            for a in range(3)
        ]
        q = d[0] * d[0] + d[1] * d[1] + d[2] * d[2]
        if on_diagonal:
            row_label = start + lax.broadcasted_iota(jnp.int32, (16, LANES), 0)
            col_label = tile * LANES + lax.broadcasted_iota(jnp.int32, (16, LANES), 1)
            retain = row_label != col_label
            q = jnp.where(retain, q, 4.0)
        u = lax.rsqrt(q)
        r = q * u
        near = r < 2.0
        u2 = u * u
        f = jnp.where(near, 1.0 - 0.28125 * r, u * (0.75 + 0.5 * u2))
        if on_diagonal:
            f = jnp.where(retain, f, 0.0)
        h = u * jnp.where(near, 0.09375, u2 * (0.75 - 1.5 * u2))
        hd = [h * d[a] for a in range(3)]
        for n, (a, b) in enumerate(BLOCKS):
            element = hd[a] * d[b]
            if a == b:
                element = element + f
            mobility[n, tile, at_rows, :] = element.astype(bf16)

    def rows_of(b):
        return pl.ds(b * samples, samples)

    def lanes_of(span):
        return pl.ds(span[0] * LANES, (span[1] - span[0]) * LANES)

    def fold(x):
        x = x[:samples] + x[samples : 2 * samples] + x[2 * samples :]
        parts = [x[:, start : start + LANES] for start in range(0, x.shape[1], LANES)]
        return functools.reduce(jnp.add, parts)

    def total(x):
        return jnp.sum(x, axis=1, keepdims=True)

    def total_row(x):
        return jnp.sum(jnp.transpose(x), axis=0, keepdims=True)

    def thrice(x):
        return jnp.concatenate([x, x, x], axis=0)

    def spread(pieces):
        zero = jnp.zeros_like(pieces[0])
        columns = []
        for a, b in BLOCKS:
            column = [zero, zero, zero]
            column[a], column[b] = pieces[b], pieces[a]
            columns.append(jnp.concatenate(column, axis=0))
        return jnp.concatenate(columns, axis=1)

    def onto_wide(pieces, span, tile):
        right = jnp.concatenate([mobility[n, tile, lanes_of(span), :] for n in range(6)], axis=0)
        return jnp.dot(spread(pieces), right, preferred_element_type=f32)

    def back(pieces, other, tile):
        at = lanes_of((other, other + 1))
        right = jnp.concatenate([mobility[n, tile, at, :] for n in range(6)], axis=1)
        return lax.dot_general(
            spread(pieces), right, (((1,), (1,)), ((), ())), preferred_element_type=f32
        )

    def blockwise(pieces, dot):
        sums = [None] * 3
        for n, (a, b) in enumerate(BLOCKS):
            if a == b:
                parts = [(a, dot(pieces[a], n))]
            else:
                part = dot(jnp.concatenate([pieces[b], pieces[a]], axis=0), n)
                parts = [(a, part[:samples]), (b, part[samples:])]
            for c, part in parts:
                sums[c] = part if sums[c] is None else sums[c] + part
        return jnp.concatenate(sums, axis=0)

    def onto(pieces, span, tile):
        def dot(left, n):
            right = mobility[n, tile, lanes_of(span), :]
            return jnp.dot(left, right, preferred_element_type=f32)

        return blockwise(pieces, dot)

    def noise_pieces(span):
        return [narrow[rows_of(b), lanes_of(span)] for b in range(3)]

    own_turned = jnp.transpose(own_ref[...])

    def members(tile):
        return order[tile * per_tile : (tile + 1) * per_tile]

    def receive(tile):
        at = pl.ds(tile * LANES, LANES)
        blocks = 2 * per_tile
        first = max(tile * blocks, 1)
        finished(gathered.at[pl.ds(first, (tile + 1) * blocks - first)], recv_sem.at[tile])
        packed = gathered[pl.ds(tile * blocks, blocks)].reshape(LANES, LANES)
        pos_cols[at, :] = jnp.dot(packed, over_lanes, preferred_element_type=f32)
        turned = lax.dot_general(
            turning, packed, (((1,), (1,)), ((), ())), preferred_element_type=f32
        )
        pos_rows[:, at] = turned[fields:]
        noise_full[:, at] = turned[:fields]
        narrow[:, at] = turned[:fields].astype(bf16)
        if tile == 0:
            noise_full[:, pl.ds(0, per_device)] = own_turned[:fields]

    for group in range(chips // SHARED):
        send_later(group)
    def spread_products(tile, others, gained=None):
        for other in others:
            part = onto_wide(noise_pieces((other, other + 1)), (other, other + 1), tile)
            gained = part if gained is None else gained + part
            if other < tile:
                at = lanes_of((other, other + 1))
                image[:, at] = image[:, at] + back(noise_pieces((tile, tile + 1)), other, tile)
        return gained

    held = []
    for tile in range(tiles):
        receive(tile)
        for late in held:
            image[:, lanes_of((late, late + 1))] = spread_products(late, range(late + 1))
        held = []
        gained = None
        for other in range(tile + 1):
            for step in range(LANES // 16):
                form(other * LANES + step * 16, tile, other == tile)
            if tile not in range(tiles - 2, tiles - 1):
                gained = spread_products(tile, [other], gained)
        if tile in range(tiles - 2, tiles - 1):
            held.append(tile)
        else:
            image[:, lanes_of((tile, tile + 1))] = gained

    square_parts = fold(noise_full[...] * noise_full[...])
    inverse = 1.0 / (total(square_parts) + 1e-06)
    first_image = image[...]
    coupled_parts = fold(noise_full[...] * first_image)
    slope = (total(coupled_parts) - 1e-06) * inverse
    remainder = first_image - thrice(slope) * noise_full[...]
    remainders = fold(remainder * remainder)

    rounded = remainder.astype(bf16)
    twice = rounded + rounded
    parts = remainders
    for tile in range(tiles):
        at = slice(tile * LANES, (tile + 1) * LANES)
        pieces = []
        for b in range(3):
            rows_at = slice(b * samples, (b + 1) * samples)
            piece = rounded[rows_at, at]
            if tile:
                piece = jnp.concatenate([twice[rows_at, : tile * LANES], piece], axis=1)
            pieces.append(piece)
        parts = parts + fold(remainder[:, at] * onto(pieces, (0, tile + 1), tile))

    squares, coupled = total_row(square_parts), total_row(coupled_parts)
    inverse = 1.0 / (squares + 1e-06)
    alpha_one = (squares + coupled) * inverse
    beta_squared = total_row(remainders) * inverse + 1e-06
    ratio = inverse / beta_squared
    own_remainder = jnp.transpose(remainder[:, :LANES])[:per_device]
    alpha_two = total_row(parts) * ratio
    det_root = jnp.sqrt(alpha_one * alpha_two - beta_squared)
    trace_root = jnp.sqrt(alpha_one + alpha_two + 2.0 * det_root)
    scale = 0.5 / trace_root
    weight = (alpha_one + det_root) * scale
    for b in range(3):
        own = own_remainder[:, b * samples : (b + 1) * samples]
        out_ref[b] = weight * noise_ref[b] + scale * own

    finished(gathered.at[pl.ds(1, 2 * chips - 1)], send_sem.at[0])


def replicated(mesh, positions, thermal_noise):
    rows, cols = mesh.shape["row"], mesh.shape["col"]
    samples, _, per_device = thermal_noise.shape
    particles = rows * cols * per_device
    chips = rows * cols // 2
    f32, bf16 = jnp.float32, jnp.bfloat16
    vmem = pl.BlockSpec(memory_space=pltpu.VMEM)
    anywhere = pl.BlockSpec(memory_space=pl.ANY)
    out = pl.pallas_call(
        functools.partial(replicated_kernel, rows, cols),
        out_shape=pltpu.VMEM((3, per_device, samples), f32),
        in_specs=[anywhere, anywhere],
        out_specs=vmem,
        scratch_shapes=[
            pltpu.VMEM((3, per_device, samples), f32),
            pltpu.VMEM((3, per_device), f32),
            pltpu.VMEM((2 * chips, per_device, LANES), bf16),
            pltpu.VMEM((16, LANES), f32),
            pltpu.VMEM((per_device, LANES), f32),
            pltpu.VMEM((3 * samples, particles), f32),
            pltpu.VMEM((particles, 3 * LANES), f32),
            pltpu.VMEM((3 * 16, particles), f32),
            pltpu.VMEM((6, particles // LANES, particles, LANES), bf16),
            pltpu.VMEM((3 * samples, particles), bf16),
            pltpu.VMEM((3 * samples, particles), f32),
            pltpu.SemaphoreType.DMA((2,)),
            pltpu.SemaphoreType.DMA((1,)),
            pltpu.SemaphoreType.DMA((particles // LANES,)),
            pltpu.SemaphoreType.REGULAR((chips // SHARED,)),
        ],
        compiler_params=pltpu.CompilerParams(collective_id=0, has_side_effects=True),
        name="lanczos",
    )(jnp.transpose(thermal_noise, (1, 2, 0)), positions)
    return jnp.transpose(out, (2, 0, 1))


def fits(mesh, positions, thermal_noise):
    rows, cols = mesh.shape["row"], mesh.shape["col"]
    samples, _, particles = thermal_noise.shape
    per_device = particles // (rows * cols)
    return (
        rows & (rows - 1) == 0
        and cols & (cols - 1) == 0
        and min(rows, cols) >= 2
        and 4 * samples == LANES
        and per_device == 16
        and particles % (2 * LANES) == 0
        and 12 * particles * particles <= 2**24
    )


def pair_tensor(rows_pos, cols_pos, retain):
    offsets = [rows_pos[a][None, :] - cols_pos[a][:, None] for a in range(3)]
    squared = offsets[0] * offsets[0] + offsets[1] * offsets[1] + offsets[2] * offsets[2]
    guarded = jnp.where(retain, squared, 4.0)
    inverse = lax.rsqrt(guarded)
    distance = guarded * inverse
    correlation = distance < 2.0
    inverse_cube = inverse * inverse * inverse
    inverse_fifth = inverse_cube * inverse * inverse
    isotropic = jnp.where(
        correlation, 1.0 - 0.28125 * distance, 0.75 * inverse + 0.5 * inverse_cube
    )
    dyadic = jnp.where(correlation, 0.09375 * inverse, 0.75 * inverse_cube - 1.5 * inverse_fifth)
    isotropic = jnp.where(retain, isotropic, 0.0)
    dyadic = jnp.where(retain, dyadic, 0.0)
    columns = []
    for b in range(3):
        elements = []
        for a in range(3):
            element = dyadic * offsets[a] * offsets[b]
            if a == b:
                element = element + isotropic
            elements.append(element)
        columns.append(jnp.stack(elements, axis=1))
    return jnp.stack(columns, axis=0)


def half_image(pos_rows, pos_cols, vec_rows, vec_cols, own_vector):
    row_devices = lax.axis_size("row")
    col_devices = lax.axis_size("col")
    row_index = lax.axis_index("row")
    col_index = lax.axis_index("col")
    samples = own_vector.shape[0]
    per_device = own_vector.shape[2]
    row_count = pos_rows.shape[1]
    row_label = row_index * col_devices * per_device + lax.iota(jnp.int32, row_count)
    group_size = min(row_devices, max(1, 128 // per_device))
    width = group_size * per_device
    group_count = row_devices // group_size
    sum_rows = jnp.zeros((samples, 3, row_count), jnp.float32)
    sum_cols = jnp.zeros((samples, 3, per_device * row_devices), jnp.float32)

    def add_group(group, totals):
        sum_rows, sum_cols = totals
        start = group * width
        cols_pos = lax.dynamic_slice_in_dim(pos_cols, start, width, 1)
        cols_vec = lax.dynamic_slice_in_dim(vec_cols, start, width, 2)
        local_cols = lax.iota(jnp.int32, width)
        segment = group * group_size + local_cols // per_device
        col_label = (segment * col_devices + col_index) * per_device + local_cols % per_device
        keep = segment >= row_index
        upper = (segment != row_index)[:, None] | (row_label[None, :] < col_label[:, None])
        retain = keep[:, None] & upper & (row_label[None, :] != col_label[:, None])
        tensor = pair_tensor(pos_rows, cols_pos, retain).astype(jnp.bfloat16)
        sum_rows = sum_rows + jnp.einsum(
            "kbj,bjai->kai", cols_vec, tensor, preferred_element_type=jnp.float32
        )
        credit = jnp.einsum("kai,bjai->kbj", vec_rows, tensor, preferred_element_type=jnp.float32)
        previous = lax.dynamic_slice_in_dim(sum_cols, start, width, 2)
        sum_cols = lax.dynamic_update_slice_in_dim(sum_cols, previous + credit, start, 2)
        return (sum_rows, sum_cols)

    totals = (sum_rows, sum_cols)
    totals = lax.fori_loop(row_index // group_size, group_count, add_group, totals)
    sum_rows, sum_cols = totals
    mobility_image = own_vector + lax.psum_scatter(sum_rows, "col", scatter_dimension=2, tiled=True)
    return mobility_image + lax.psum_scatter(sum_cols, "row", scatter_dimension=2, tiled=True)


def on_device(positions, thermal_noise):
    squares = lax.psum(jnp.sum(thermal_noise * thermal_noise, axis=(1, 2)), ("row", "col"))
    noise_length = jnp.sqrt(squares + 1e-06)
    basis_one = thermal_noise / noise_length[:, None, None]
    pos_cols, cols_one = (
        lax.all_gather(positions, "row", axis=1, tiled=True),
        lax.all_gather(basis_one, "row", axis=2, tiled=True),
    )
    pos_rows, rows_wide = (
        lax.all_gather(positions, "col", axis=1, tiled=True),
        lax.all_gather(basis_one, "col", axis=2, tiled=True),
    )
    image_one = half_image(
        pos_rows, pos_cols, rows_wide.astype(jnp.bfloat16), cols_one.astype(jnp.bfloat16), basis_one
    )
    alpha_one = lax.psum(jnp.sum(basis_one * image_one, axis=(1, 2)), ("row", "col"))
    remainder = image_one - alpha_one[:, None, None] * basis_one
    beta_squared = lax.psum(jnp.sum(remainder * remainder, axis=(1, 2)), ("row", "col"))
    beta_one = jnp.sqrt(beta_squared + 1e-06)
    basis_two = remainder / beta_one[:, None, None]
    narrow_two = basis_two.astype(jnp.bfloat16)
    cols_two = lax.all_gather(narrow_two, "row", axis=2, tiled=True)
    rows_two = lax.all_gather(narrow_two, "col", axis=2, tiled=True)
    image_two = half_image(pos_rows, pos_cols, rows_two, cols_two, basis_two)
    alpha_two = lax.psum(jnp.sum(basis_two * image_two, axis=(1, 2)), ("row", "col"))
    det_root = jnp.sqrt(alpha_one * alpha_two - beta_one * beta_one)
    trace_root = jnp.sqrt(alpha_one + alpha_two + 2.0 * det_root)
    weight_one = (alpha_one + det_root) / trace_root
    weight_two = beta_one / trace_root
    return (
        0.5
        * noise_length[:, None, None]
        * (weight_one[:, None, None] * basis_one + weight_two[:, None, None] * basis_two)
    )


def solution(mesh):
    specs = dict(
        mesh=mesh,
        in_specs=(P(None, ("row", "col")), P(None, None, ("row", "col"))),
        out_specs=P(None, None, ("row", "col")),
        check_vma=False,
    )

    def program(positions, thermal_noise):
        if fits(mesh, positions, thermal_noise):
            body = functools.partial(replicated, mesh)
        else:
            body = on_device
        return jax.shard_map(body, **specs)(positions, thermal_noise)

    return program
```

```python
import functools

import jax
import jax.numpy as jnp
from jax import lax
from jax.experimental import pallas as pl
from jax.experimental.pallas import tpu as pltpu
from jax.sharding import PartitionSpec as P

LANES = 128
SHARED = 2
LOGICAL = pl.DeviceIdType.LOGICAL
BLOCKS = ((0, 0), (1, 1), (2, 2), (0, 1), (0, 2), (1, 2))


def chip_bits(rows, cols):
    bits = [(1, 1)]
    weight = 2
    while weight < rows:
        bits.append((weight * cols, weight // 2))
        weight = 2 * weight
    weight = 2
    while weight < cols:
        bits.append((weight, weight // 2))
        weight = 2 * weight
    return bits


def replicated_kernel(
    rows,
    cols,
    noise_hbm,
    pos_hbm,
    out_ref,
    noise_ref,
    pos_ref,
    gathered,
    stage,
    own_ref,
    noise_full,
    pos_cols,
    pos_rows,
    mobility,
    narrow,
    image,
    load_sem,
    send_sem,
    recv_sem,
    grant,
):
    _, per_device, samples = noise_ref.shape
    particles = rows * cols * per_device
    f32, bf16 = jnp.float32, jnp.bfloat16
    my_row, my_col = lax.axis_index("row"), lax.axis_index("col")

    load_pos = pltpu.make_async_copy(pos_hbm, pos_ref, load_sem.at[0])
    load_noise = pltpu.make_async_copy(noise_hbm, noise_ref, load_sem.at[1])
    load_pos.start()
    load_noise.start()

    bits = chip_bits(rows, cols)
    chips = rows * cols // 2
    me = my_row * cols + my_col
    core = lax.rem(my_row, 2)
    mate = cols * (1 - 2 * core)
    my_code = 0
    device, ahead, level = {0: me}, {0: 0}, {0: 0}
    for index, (weight, height) in enumerate(bits):
        step = 19 if 2 <= weight < cols else 20
        height = height * step * chips + (1 << index)
        digit = lax.rem(me // weight, 2)
        my_code = my_code + (digit << index)
        sign = 1 - 2 * digit
        for code in range(1 << index):
            device[code + (1 << index)] = device[code] + weight * sign
            ahead[code + (1 << index)] = ahead[code] + height * sign
            level[code + (1 << index)] = level[code] + height
    order = sorted(range(chips), key=lambda code: (level[code], code))
    place = {code: index for index, code in enumerate(order)}
    my_place = 0
    for code in order[1:]:
        my_place = my_place + jnp.where(my_code == code, place[code], 0)
    per_tile = LANES // (2 * per_device)

    def both(code):
        return device[code], device[code] + mate

    barrier = pltpu.get_barrier_semaphore()
    pl.semaphore_signal(barrier, inc=1, device_id=me + mate, device_id_type=LOGICAL)
    greetings = 1
    for code in order[1:]:
        greetings = greetings + jnp.where(ahead[code] < 0, 2, 0)

        @pl.when(ahead[code] > 0)
        def _(code=code):
            for target in both(code):
                pl.semaphore_signal(barrier, inc=1, device_id=target, device_id_type=LOGICAL)

    stage[...] = jnp.zeros_like(stage)
    load_pos.wait()
    position = pos_ref[...]
    for term in range(3):
        piece = position.astype(bf16).astype(f32)
        stage[pl.ds(3 * term, 3), pl.ds(0, per_device)] = piece
        position = position - piece
    turned = jnp.transpose(stage[...])

    load_noise.wait()
    tail = jnp.zeros((per_device, LANES - 3 * samples - 16), f32)
    own = [noise_ref[b] for b in range(3)] + [turned[0:per_device, :], tail]
    own = jnp.concatenate(own, axis=1)
    gathered[0] = own.astype(bf16)
    own_ref[...] = own

    pl.semaphore_wait(barrier, greetings)

    def send(spot, side, target):
        pltpu.make_async_remote_copy(
            src_ref=gathered.at[0],
            dst_ref=gathered.at[2 * spot + side],
            send_sem=send_sem.at[0],
            recv_sem=recv_sem.at[spot // per_tile],
            device_id=target,
            device_id_type=LOGICAL,
        ).start()

    def finished(ref, semaphore):
        pltpu.make_async_copy(ref, ref, semaphore).wait()

    @pl.when(my_code > 0)
    def _():
        send(my_place, core, 0)
        send(my_place, 1 - core, cols)

    for code in order[:0:-1]:

        @pl.when(ahead[code] < 0)
        def _(code=code):
            for target in both(code):
                pl.semaphore_signal(
                    grant.at[place[code] // SHARED], inc=1, device_id=target, device_id_type=LOGICAL
                )

    for code in order[:0:-1]:

        @pl.when((ahead[code] < 0) & (my_code != code))
        def _(code=code):
            for side, target in enumerate(both(code)):
                send(place[code], side, target)

    send(0, 1, me + mate)

    def send_later(group):
        codes = [code for code in order[group * SHARED : (group + 1) * SHARED] if code]
        owed = 0
        for code in codes:
            owed = owed + jnp.where(ahead[code] > 0, 2, 0)

        @pl.when(owed > 0)
        def _():
            pl.semaphore_wait(grant.at[group], owed)
            for code in codes:

                @pl.when(ahead[code] > 0)
                def _(code=code):
                    for side, target in enumerate(both(code)):
                        send(place[code], side, target)

    lane = lax.broadcasted_iota(jnp.int32, (1, LANES), 1)
    field = lax.broadcasted_iota(jnp.int32, (LANES, 3 * LANES), 0) - 3 * samples
    target = lax.broadcasted_iota(jnp.int32, (LANES, 3 * LANES), 1) // LANES
    select = (field == target) | (field == target + 3) | (field == target + 6)
    over_lanes = select.astype(f32).astype(bf16)
    fields = 3 * samples
    field = lax.broadcasted_iota(jnp.int32, (fields + 3 * 16, LANES), 1)
    target = lax.broadcasted_iota(jnp.int32, (fields + 3 * 16, LANES), 0)
    coordinate = (target - fields) // 16
    moved = (field - fields == coordinate) | (field - fields == coordinate + 3)
    moved = moved | (field - fields == coordinate + 6)
    select = ((target < fields) & (field == target)) | ((target >= fields) & moved)
    turning = select.astype(f32).astype(bf16)
    tiles = particles // LANES

    def form(start, tile, on_diagonal):
        at_rows, at_lanes = pl.ds(start, 16), pl.ds(tile * LANES, LANES)
        d = [
            pos_cols[at_rows, pl.ds(a * LANES, LANES)] - pos_rows[pl.ds(a * 16, 16), at_lanes]
            for a in range(3)
        ]
        q = d[0] * d[0] + d[1] * d[1] + d[2] * d[2]
        if on_diagonal:
            row_label = start + lax.broadcasted_iota(jnp.int32, (16, LANES), 0)
            col_label = tile * LANES + lax.broadcasted_iota(jnp.int32, (16, LANES), 1)
            retain = row_label != col_label
            q = jnp.where(retain, q, 4.0)
        u = lax.rsqrt(q)
        r = q * u
        near = r < 2.0
        u2 = u * u
        f = jnp.where(near, 1.0 - 0.28125 * r, u * (0.75 + 0.5 * u2))
        if on_diagonal:
            f = jnp.where(retain, f, 0.0)
        h = u * jnp.where(near, 0.09375, u2 * (0.75 - 1.5 * u2))
        hd = [h * d[a] for a in range(3)]
        for n, (a, b) in enumerate(BLOCKS):
            element = hd[a] * d[b]
            if a == b:
                element = element + f
            mobility[n, tile, at_rows, :] = element.astype(bf16)

    def rows_of(b):
        return pl.ds(b * samples, samples)

    def lanes_of(span):
        return pl.ds(span[0] * LANES, (span[1] - span[0]) * LANES)

    def fold(x):
        x = x[:samples] + x[samples : 2 * samples] + x[2 * samples :]
        parts = [x[:, start : start + LANES] for start in range(0, x.shape[1], LANES)]
        return functools.reduce(jnp.add, parts)

    def total(x):
        return jnp.sum(x, axis=1, keepdims=True)

    def total_row(x):
        return jnp.sum(jnp.transpose(x), axis=0, keepdims=True)

    def thrice(x):
        return jnp.concatenate([x, x, x], axis=0)

    def spread(pieces):
        zero = jnp.zeros_like(pieces[0])
        columns = []
        for a, b in BLOCKS:
            column = [zero, zero, zero]
            column[a], column[b] = pieces[b], pieces[a]
            columns.append(jnp.concatenate(column, axis=0))
        return jnp.concatenate(columns, axis=1)

    def onto_wide(pieces, span, tile):
        right = jnp.concatenate([mobility[n, tile, lanes_of(span), :] for n in range(6)], axis=0)
        return jnp.dot(spread(pieces), right, preferred_element_type=f32)

    def back(pieces, other, tile):
        at = lanes_of((other, other + 1))
        right = jnp.concatenate([mobility[n, tile, at, :] for n in range(6)], axis=1)
        return lax.dot_general(
            spread(pieces), right, (((1,), (1,)), ((), ())), preferred_element_type=f32
        )

    def blockwise(pieces, dot):
        sums = [None] * 3
        for n, (a, b) in enumerate(BLOCKS):
            if a == b:
                parts = [(a, dot(pieces[a], n))]
            else:
                part = dot(jnp.concatenate([pieces[b], pieces[a]], axis=0), n)
                parts = [(a, part[:samples]), (b, part[samples:])]
            for c, part in parts:
                sums[c] = part if sums[c] is None else sums[c] + part
        return jnp.concatenate(sums, axis=0)

    def onto(pieces, span, tile):
        def dot(left, n):
            right = mobility[n, tile, lanes_of(span), :]
            return jnp.dot(left, right, preferred_element_type=f32)

        return blockwise(pieces, dot)

    def noise_pieces(span):
        return [narrow[rows_of(b), lanes_of(span)] for b in range(3)]

    own_turned = jnp.transpose(own_ref[...])

    def members(tile):
        return order[tile * per_tile : (tile + 1) * per_tile]

    def receive(tile):
        at = pl.ds(tile * LANES, LANES)
        blocks = 2 * per_tile
        first = max(tile * blocks, 1)
        finished(gathered.at[pl.ds(first, (tile + 1) * blocks - first)], recv_sem.at[tile])
        packed = gathered[pl.ds(tile * blocks, blocks)].reshape(LANES, LANES)
        pos_cols[at, :] = jnp.dot(packed, over_lanes, preferred_element_type=f32)
        turned = lax.dot_general(
            turning, packed, (((1,), (1,)), ((), ())), preferred_element_type=f32
        )
        pos_rows[:, at] = turned[fields:]
        noise_full[:, at] = turned[:fields]
        narrow[:, at] = turned[:fields].astype(bf16)
        if tile == 0:
            noise_full[:, pl.ds(0, per_device)] = own_turned[:fields]

    for group in range(chips // SHARED):
        send_later(group)
    def spread_products(tile, others, gained=None):
        for other in others:
            part = onto_wide(noise_pieces((other, other + 1)), (other, other + 1), tile)
            gained = part if gained is None else gained + part
            if other < tile:
                at = lanes_of((other, other + 1))
                image[:, at] = image[:, at] + back(noise_pieces((tile, tile + 1)), other, tile)
        return gained

    held = []
    for tile in range(tiles):
        receive(tile)
        for late in held:
            image[:, lanes_of((late, late + 1))] = spread_products(late, range(late + 1))
        held = []
        gained = None
        for other in range(tile + 1):
            for step in range(LANES // 16):
                form(other * LANES + step * 16, tile, other == tile)
            if tile not in range(tiles - 2, tiles - 1):
                gained = spread_products(tile, [other], gained)
        if tile in range(tiles - 2, tiles - 1):
            held.append(tile)
        else:
            image[:, lanes_of((tile, tile + 1))] = gained

    square_parts = fold(noise_full[...] * noise_full[...])
    inverse = 1.0 / (total(square_parts) + 1e-06)
    first_image = image[...]
    coupled_parts = fold(noise_full[...] * first_image)
    slope = (total(coupled_parts) - 1e-06) * inverse
    remainder = first_image - thrice(slope) * noise_full[...]
    remainders = fold(remainder * remainder)

    rounded = remainder.astype(bf16)
    twice = rounded + rounded
    parts = remainders
    for tile in range(tiles):
        at = slice(tile * LANES, (tile + 1) * LANES)
        pieces = []
        for b in range(3):
            rows_at = slice(b * samples, (b + 1) * samples)
            piece = rounded[rows_at, at]
            if tile:
                piece = jnp.concatenate([twice[rows_at, : tile * LANES], piece], axis=1)
            pieces.append(piece)
        parts = parts + fold(remainder[:, at] * onto(pieces, (0, tile + 1), tile))

    squares, coupled = total_row(square_parts), total_row(coupled_parts)
    inverse = 1.0 / (squares + 1e-06)
    alpha_one = (squares + coupled) * inverse
    beta_squared = total_row(remainders) * inverse + 1e-06
    ratio = inverse / beta_squared
    own_remainder = jnp.transpose(remainder[:, :LANES])[:per_device]
    alpha_two = total_row(parts) * ratio
    det_root = jnp.sqrt(alpha_one * alpha_two - beta_squared)
    trace_root = jnp.sqrt(alpha_one + alpha_two + 2.0 * det_root)
    scale = 0.5 / trace_root
    weight = (alpha_one + det_root) * scale
    for b in range(3):
        own = own_remainder[:, b * samples : (b + 1) * samples]
        out_ref[b] = weight * noise_ref[b] + scale * own

    finished(gathered.at[pl.ds(1, 2 * chips - 1)], send_sem.at[0])


def replicated(mesh, positions, thermal_noise):
    rows, cols = mesh.shape["row"], mesh.shape["col"]
    samples, _, per_device = thermal_noise.shape
    particles = rows * cols * per_device
    chips = rows * cols // 2
    f32, bf16 = jnp.float32, jnp.bfloat16
    vmem = pl.BlockSpec(memory_space=pltpu.VMEM)
    anywhere = pl.BlockSpec(memory_space=pl.ANY)
    out = pl.pallas_call(
        functools.partial(replicated_kernel, rows, cols),
        out_shape=pltpu.VMEM((3, per_device, samples), f32),
        in_specs=[anywhere, anywhere],
        out_specs=vmem,
        scratch_shapes=[
            pltpu.VMEM((3, per_device, samples), f32),
            pltpu.VMEM((3, per_device), f32),
            pltpu.VMEM((2 * chips, per_device, LANES), bf16),
            pltpu.VMEM((16, LANES), f32),
            pltpu.VMEM((per_device, LANES), f32),
            pltpu.VMEM((3 * samples, particles), f32),
            pltpu.VMEM((particles, 3 * LANES), f32),
            pltpu.VMEM((3 * 16, particles), f32),
            pltpu.VMEM((6, particles // LANES, particles, LANES), bf16),
            pltpu.VMEM((3 * samples, particles), bf16),
            pltpu.VMEM((3 * samples, particles), f32),
            pltpu.SemaphoreType.DMA((2,)),
            pltpu.SemaphoreType.DMA((1,)),
            pltpu.SemaphoreType.DMA((particles // LANES,)),
            pltpu.SemaphoreType.REGULAR((chips // SHARED,)),
        ],
        compiler_params=pltpu.CompilerParams(collective_id=0, has_side_effects=True),
        name="lanczos",
    )(jnp.transpose(thermal_noise, (1, 2, 0)), positions)
    return jnp.transpose(out, (2, 0, 1))


def fits(mesh, positions, thermal_noise):
    rows, cols = mesh.shape["row"], mesh.shape["col"]
    samples, _, particles = thermal_noise.shape
    per_device = particles // (rows * cols)
    return (
        rows & (rows - 1) == 0
        and cols & (cols - 1) == 0
        and min(rows, cols) >= 2
        and 4 * samples == LANES
        and per_device == 16
        and particles % (2 * LANES) == 0
        and 12 * particles * particles <= 2**24
    )


def pair_tensor(rows_pos, cols_pos, retain):
    offsets = [rows_pos[a][None, :] - cols_pos[a][:, None] for a in range(3)]
    squared = offsets[0] * offsets[0] + offsets[1] * offsets[1] + offsets[2] * offsets[2]
    guarded = jnp.where(retain, squared, 4.0)
    inverse = lax.rsqrt(guarded)
    distance = guarded * inverse
    correlation = distance < 2.0
    inverse_cube = inverse * inverse * inverse
    inverse_fifth = inverse_cube * inverse * inverse
    isotropic = jnp.where(
        correlation, 1.0 - 0.28125 * distance, 0.75 * inverse + 0.5 * inverse_cube
    )
    dyadic = jnp.where(correlation, 0.09375 * inverse, 0.75 * inverse_cube - 1.5 * inverse_fifth)
    isotropic = jnp.where(retain, isotropic, 0.0)
    dyadic = jnp.where(retain, dyadic, 0.0)
    columns = []
    for b in range(3):
        elements = []
        for a in range(3):
            element = dyadic * offsets[a] * offsets[b]
            if a == b:
                element = element + isotropic
            elements.append(element)
        columns.append(jnp.stack(elements, axis=1))
    return jnp.stack(columns, axis=0)


def half_image(pos_rows, pos_cols, vec_rows, vec_cols, own_vector):
    row_devices = lax.axis_size("row")
    col_devices = lax.axis_size("col")
    row_index = lax.axis_index("row")
    col_index = lax.axis_index("col")
    samples = own_vector.shape[0]
    per_device = own_vector.shape[2]
    row_count = pos_rows.shape[1]
    row_label = row_index * col_devices * per_device + lax.iota(jnp.int32, row_count)
    group_size = min(row_devices, max(1, 128 // per_device))
    width = group_size * per_device
    group_count = row_devices // group_size
    sum_rows = jnp.zeros((samples, 3, row_count), jnp.float32)
    sum_cols = jnp.zeros((samples, 3, per_device * row_devices), jnp.float32)

    def add_group(group, totals):
        sum_rows, sum_cols = totals
        start = group * width
        cols_pos = lax.dynamic_slice_in_dim(pos_cols, start, width, 1)
        cols_vec = lax.dynamic_slice_in_dim(vec_cols, start, width, 2)
        local_cols = lax.iota(jnp.int32, width)
        segment = group * group_size + local_cols // per_device
        col_label = (segment * col_devices + col_index) * per_device + local_cols % per_device
        keep = segment >= row_index
        upper = (segment != row_index)[:, None] | (row_label[None, :] < col_label[:, None])
        retain = keep[:, None] & upper & (row_label[None, :] != col_label[:, None])
        tensor = pair_tensor(pos_rows, cols_pos, retain).astype(jnp.bfloat16)
        sum_rows = sum_rows + jnp.einsum(
            "kbj,bjai->kai", cols_vec, tensor, preferred_element_type=jnp.float32
        )
        credit = jnp.einsum("kai,bjai->kbj", vec_rows, tensor, preferred_element_type=jnp.float32)
        previous = lax.dynamic_slice_in_dim(sum_cols, start, width, 2)
        sum_cols = lax.dynamic_update_slice_in_dim(sum_cols, previous + credit, start, 2)
        return (sum_rows, sum_cols)

    totals = (sum_rows, sum_cols)
    totals = lax.fori_loop(row_index // group_size, group_count, add_group, totals)
    sum_rows, sum_cols = totals
    mobility_image = own_vector + lax.psum_scatter(sum_rows, "col", scatter_dimension=2, tiled=True)
    return mobility_image + lax.psum_scatter(sum_cols, "row", scatter_dimension=2, tiled=True)


def on_device(positions, thermal_noise):
    squares = lax.psum(jnp.sum(thermal_noise * thermal_noise, axis=(1, 2)), ("row", "col"))
    noise_length = jnp.sqrt(squares + 1e-06)
    basis_one = thermal_noise / noise_length[:, None, None]
    pos_cols, cols_one = (
        lax.all_gather(positions, "row", axis=1, tiled=True),
        lax.all_gather(basis_one, "row", axis=2, tiled=True),
    )
    pos_rows, rows_wide = (
        lax.all_gather(positions, "col", axis=1, tiled=True),
        lax.all_gather(basis_one, "col", axis=2, tiled=True),
    )
    image_one = half_image(
        pos_rows, pos_cols, rows_wide.astype(jnp.bfloat16), cols_one.astype(jnp.bfloat16), basis_one
    )
    alpha_one = lax.psum(jnp.sum(basis_one * image_one, axis=(1, 2)), ("row", "col"))
    remainder = image_one - alpha_one[:, None, None] * basis_one
    beta_squared = lax.psum(jnp.sum(remainder * remainder, axis=(1, 2)), ("row", "col"))
    beta_one = jnp.sqrt(beta_squared + 1e-06)
    basis_two = remainder / beta_one[:, None, None]
    narrow_two = basis_two.astype(jnp.bfloat16)
    cols_two = lax.all_gather(narrow_two, "row", axis=2, tiled=True)
    rows_two = lax.all_gather(narrow_two, "col", axis=2, tiled=True)
    image_two = half_image(pos_rows, pos_cols, rows_two, cols_two, basis_two)
    alpha_two = lax.psum(jnp.sum(basis_two * image_two, axis=(1, 2)), ("row", "col"))
    det_root = jnp.sqrt(alpha_one * alpha_two - beta_one * beta_one)
    trace_root = jnp.sqrt(alpha_one + alpha_two + 2.0 * det_root)
    weight_one = (alpha_one + det_root) / trace_root
    weight_two = beta_one / trace_root
    return (
        0.5
        * noise_length[:, None, None]
        * (weight_one[:, None, None] * basis_one + weight_two[:, None, None] * basis_two)
    )


def solution(mesh):
    specs = dict(
        mesh=mesh,
        in_specs=(P(None, ("row", "col")), P(None, None, ("row", "col"))),
        out_specs=P(None, None, ("row", "col")),
        check_vma=False,
    )

    def program(positions, thermal_noise):
        if fits(mesh, positions, thermal_noise):
            body = functools.partial(replicated, mesh)
        else:
            body = on_device
        return jax.shard_map(body, **specs)(positions, thermal_noise)

    return program
```
